256 devices in a mesh: ent: 32 (over y, z), dim: 8 (over x, core).
Axes of the slice: x: 4, y: 4, z: 8, core: 2. Of those that a mesh axis runs over, the one named last changes fastest.
Arguments:
- entities: float32 [65536, 1024], P('ent', 'dim'), may hold values from -3 to 3
- ent_state: float32 [65536], P('ent'), may hold values from 0.01 to 0.1
- buckets: int32 [65536], P('ent'), may hold values from 0 to 7
- relations: float32 [4096, 1024], P(None, 'dim'), may hold values from -1.6 to 1.6
- rel_state: float32 [4096], replicated, may hold values from 0.05 to 0.5
- triples: int32 [3, 16384], P(None, 'ent'), may hold values from 0 to 65535, as said below
- negatives: int32 [64, 256], P('ent'), may hold values from 0 to 65535, as said below
Outputs:
- new_entities: float32 [65536, 1024], P('ent', 'dim')
- new_relations: float32 [4096, 1024], P(None, 'dim')
The draws below stay inside these ranges and needn't reach their ends.
Inputs may be any that keep to these rules, and one draw needn't show every extreme that they name: `triples`: rows 0 and 2 hold entity ids, row 1 relation ids below 4096. The block of an entity id is id // 2048. Among the 768 ids of one group (its heads, its tails and its negatives) at most 64 lie in one block, and in every draw, for each rank of a group among the 2 groups of an index of ent, some block holds exactly 64 ids of that group on every index of ent. `negatives`: entity ids; they count in the bound on the ids of a group stated for triples.
All inputs are finite; a program needn't handle non-finite values.
Results may differ from the reference program's by a relative error of at most 0.0017.
Values may be sent and summed in bfloat16 or wider, within the bound.
No kernel may reach another device: no remote copies, remote signals or barrier semaphores. Data moves between devices by JAX's collectives and lax.ppermute only.
A program may use at most 64 MiB of HBM per device.

```python
import math
import jax
import jax.numpy as jnp
from jax import lax

RANK = 512
BLK = 64
NREL = 4096
NEG = 256
GROUP = 256
NBUCK = 8
GROUP_DEV = 2
ENT_DEV = 2048
NENT = 65536
GROUPS = 64
TRIPLES = 16384
REQC = 768
CAPC = 64


def group_entity_ids(key):
    owner_count = NENT // ENT_DEV
    labels = jnp.repeat(jnp.arange(owner_count, dtype=jnp.int32), CAPC)
    star_owner = jax.random.randint(jax.random.fold_in(key, 11), (GROUP_DEV,), 0, owner_count)

    def one_group(group_key, full_owner):
        first_key, second_key, third_key, fourth_key = jax.random.split(group_key, 4)
        scores = jax.random.permutation(first_key, owner_count * CAPC).astype(jnp.int32)
        scores = jnp.where(labels == full_owner, scores - owner_count * CAPC, scores)
        order = jnp.argsort(scores, stable=True)
        chosen = labels[order[:REQC]]
        chosen = chosen[jax.random.permutation(second_key, REQC)]
        upper = jax.random.randint(third_key, (REQC,), 1, ENT_DEV + 1)
        local_rows = jax.random.randint(fourth_key, (REQC,), 0, upper)
        return chosen * ENT_DEV + local_rows
    group_keys = jax.random.split(jax.random.fold_in(key, 7), GROUPS)
    full_owners = star_owner[jnp.arange(GROUPS) % GROUP_DEV]
    return jax.vmap(one_group)(group_keys, full_owners).astype(jnp.int32)


def draw_triples(key, part):
    entity_ids = group_entity_ids(key)
    head_ids = entity_ids[:, :GROUP].reshape(TRIPLES)
    tail_ids = entity_ids[:, GROUP:2 * GROUP].reshape(TRIPLES)
    upper = jax.random.randint(jax.random.fold_in(key, 13), (TRIPLES,), 1, NREL + 1)
    rel_ids = jax.random.randint(jax.random.fold_in(key, 17), (TRIPLES,), 0, upper)
    return jnp.stack([head_ids, rel_ids.astype(jnp.int32), tail_ids], axis=0)


def draw_negatives(key, part):
    entity_ids = group_entity_ids(key)
    return entity_ids[:, 2 * GROUP:]


def touch_ends(values, own_key, smallest, high):
    spot = [jax.random.randint(jax.random.fold_in(own_key, axis), (), 0, length) for axis, length in enumerate(values.shape)]
    main_axis = values.shape.index(max(values.shape))
    next_to = spot[:main_axis] + [(spot[main_axis] + 1) % values.shape[main_axis]] + spot[main_axis + 1:]
    return values.at[tuple(spot)].set(smallest).at[tuple(next_to)].set(high)


def shard_levels(stream_key, extent, pieces, smallest, high):
    def one(position, blocks):
        heights = jax.random.uniform(jax.random.fold_in(jax.random.fold_in(stream_key, 6), position), (blocks,), jnp.float32, smallest / len(pieces), high / len(pieces))
        return jnp.repeat(jnp.exp(heights), extent[position] // blocks).reshape((-1,) + (1,) * (len(extent) - position - 1))

    gain = one(*pieces[0])
    for cut in pieces[1:]:
        gain = gain * one(*cut)
    return gain


def noise(key, shape, scale, bound, pieces=(), kind=jnp.bfloat16):
    array = jax.random.normal(key, shape, jnp.float32) * scale
    if len(pieces) > 0:
        array = shard_levels(key, shape, pieces, -0.22, 0.18) * array
    return jnp.clip(array, min=-bound, max=bound).astype(kind)


def setup_inputs(seed: int = 0) -> dict:
    splits = jax.random.split(jax.random.key(seed), 8)
    entities = noise(splits[0], (NENT, 2 * RANK), 0.5, 3.0, ((0, 32), (1, 8)), jnp.float32)
    ent_state = jnp.clip(jnp.exp(math.log(0.1) - 2.3025851 * jax.random.uniform(splits[1], (NENT,), jnp.float32) ** shard_levels(splits[1], (NENT,), ((0, 32),), -0.2, 0.2)), 0.01, 0.1)
    buckets = touch_ends(jax.random.randint(splits[2], (NENT,), 0, NBUCK), jax.random.fold_in(splits[2], 1), 0, NBUCK - 1).astype(jnp.int32)
    relations = noise(splits[3], (NREL, 2 * RANK), 0.27, 1.6, ((1, 8),), jnp.float32)
    rel_state = jnp.clip(jnp.exp(jax.random.uniform(splits[4], (NREL,), jnp.float32, math.log(0.05), math.log(0.5))), 0.05, 0.5)
    triples = draw_triples(jax.random.fold_in(splits[7], 71), 0)
    negatives = draw_negatives(jax.random.fold_in(splits[7], 71), 0)
    return {"entities": entities, "ent_state": ent_state, "buckets": buckets, "relations": relations, "rel_state": rel_state, "triples": triples, "negatives": negatives}


LEARN_RATE = 0.1
REG_WEIGHT = 0.01

def halves(values):
    shaped = values.reshape(values.shape[:-1] + (values.shape[-1] // (2 * BLK), 2, BLK))
    return (shaped[..., 0, :], shaped[..., 1, :])

def joined(real_part, imag_part):
    stacked = jnp.stack([real_part, imag_part], axis=-2)
    return stacked.reshape(stacked.shape[:-3] + (stacked.shape[-3] * 2 * BLK,))

def complex_product(former, latter):
    former_re, former_im = halves(former)
    latter_re, latter_im = halves(latter)
    return joined(former_re * latter_re - former_im * latter_im, former_re * latter_im + former_im * latter_re)

def conjugate(values):
    real_part, imag_part = halves(values)
    return joined(real_part, -imag_part)

def rounded_back(values):
    return lax.optimization_barrier(values.astype(jnp.bfloat16)).astype(jnp.float32)

def adagrad(table, state, grad):
    new_state = state + lax.optimization_barrier(jnp.mean(grad * grad, axis=-1))
    return table - LEARN_RATE * grad / jnp.sqrt(new_state)[:, None]

def reference(entities, ent_state, buckets, relations, rel_state, triples, negatives):
    ent_low = lax.optimization_barrier(entities.astype(jnp.bfloat16))
    rel_low = lax.optimization_barrier(relations.astype(jnp.bfloat16))
    head_ids = triples[0]
    rel_ids = triples[1]
    tail_ids = triples[2]
    head_rows = ent_low[head_ids].astype(jnp.float32)
    tail_rows = ent_low[tail_ids].astype(jnp.float32)
    rel_rows = rel_low[rel_ids].astype(jnp.float32)
    noise_rows = ent_low[negatives].astype(jnp.float32)
    query = rounded_back(complex_product(head_rows, rel_rows))
    probe = rounded_back(complex_product(conjugate(rel_rows), tail_rows))
    pos_score = lax.optimization_barrier(jnp.sum(query * tail_rows, axis=-1))
    query_groups = query.reshape(GROUPS, GROUP, 2 * RANK)
    probe_groups = probe.reshape(GROUPS, GROUP, 2 * RANK)
    tail_score = jnp.einsum('cid,cnd->cin', query_groups, noise_rows)
    head_score = jnp.einsum('cid,cnd->cin', probe_groups, noise_rows)
    pos_coef = rounded_back(-jax.nn.sigmoid(-pos_score))
    tail_coef = rounded_back(jax.nn.sigmoid(tail_score) / NEG)
    head_coef = rounded_back(jax.nn.sigmoid(head_score) / NEG)
    tail_pull = pos_coef[:, None] * tail_rows + jnp.einsum('cin,cnd->cid', tail_coef, noise_rows).reshape(TRIPLES, 2 * RANK)
    head_pull = jnp.einsum('cin,cnd->cid', head_coef, noise_rows).reshape(TRIPLES, 2 * RANK)
    head_side = pos_coef[:, None] * head_rows + head_pull
    head_grad = complex_product(conjugate(rel_rows), tail_pull).astype(jnp.bfloat16)
    tail_grad = complex_product(rel_rows, head_side).astype(jnp.bfloat16)
    noise_grad = (jnp.einsum('cin,cid->cnd', tail_coef, query_groups) + jnp.einsum('cin,cid->cnd', head_coef, probe_groups)).astype(jnp.bfloat16)
    rel_grad_rows = complex_product(conjugate(head_rows), tail_pull) + complex_product(tail_rows, conjugate(head_pull))
    all_ids = jnp.concatenate([head_ids, tail_ids, negatives.reshape(-1)]).astype(jnp.int32)
    all_grads = jnp.concatenate([head_grad, tail_grad, noise_grad.reshape(GROUPS * NEG, 2 * RANK)], axis=0).astype(jnp.float32)
    ent_grad = jnp.zeros((NENT, 2 * RANK), jnp.float32).at[all_ids].add(all_grads)
    counts = jnp.zeros((NENT,), jnp.float32).at[all_ids].add(jnp.ones(all_ids.shape, jnp.float32))
    weight = REG_WEIGHT * (buckets.astype(jnp.float32) + 1.0) * counts
    ent_grad = ent_grad + weight[:, None] * 3.0 * entities * jnp.abs(entities)
    rel_grad = jnp.zeros((NREL, 2 * RANK), jnp.float32).at[rel_ids].add(rel_grad_rows)
    return (adagrad(entities, ent_state, ent_grad), adagrad(relations, rel_state, rel_grad))
```

```python
import functools

import jax
import jax.numpy as jnp
from jax import lax
from jax.experimental import pallas as pl
from jax.experimental.pallas import tpu as pltpu
from jax.sharding import PartitionSpec as P

RANK = 512
HALF = 64
LANES = 128
LEARN_RATE = 0.1
REG_WEIGHT = 0.01
Y, Z, X, CORES = 4, 8, 4, 2
OWNERS = Y * Z
GROUP = 256
NEG = 256
REQ = 768
CAP = 64
SPLIT = 512
FOLD = 4
PART = 272
F32, BF16, I32 = jnp.float32, jnp.bfloat16, jnp.int32


VMEM = pl.BlockSpec(memory_space=pltpu.VMEM)
SMEM = pl.BlockSpec(memory_space=pltpu.SMEM)


def iota(shape, dim):
    return lax.broadcasted_iota(I32, shape, dim)


def column(row):
    return jnp.transpose(jnp.broadcast_to(row, (LANES, LANES)))


def swap(values):
    return pltpu.roll(values, HALF, 1)


def low_half(shape):
    return iota(shape, 1) < HALF


def product(former, latter, sign=1.0):
    low = low_half(former.shape)
    turned = swap(latter)
    real = jnp.where(low, latter, turned)
    imag = jnp.where(low, -sign * turned, sign * latter)
    return former * real + swap(former) * imag


def dot(a, b, dims=((1,), (0,))):
    return lax.dot_general(a, b, (dims, ((), ())), preferred_element_type=F32)


def kernel_call(body, outs, n_smem=0, scratch=(), name=None, flops=0):
    def call(*args):
        specs = [SMEM] * n_smem + [VMEM] * (len(args) - n_smem)
        return pl.pallas_call(
            body,
            out_shape=outs,
            in_specs=specs,
            out_specs=jax.tree.map(lambda _: VMEM, outs),
            scratch_shapes=list(scratch),
            name=name,
            compiler_params=pltpu.CompilerParams(vmem_limit_bytes=48 << 20),
            cost_estimate=pl.CostEstimate(
                flops=flops,
                transcendentals=0,
                bytes_accessed=sum(a.size * a.dtype.itemsize for a in args),
            ),
        )(*args)

    return call


def shape(dims, kind):
    return jax.ShapeDtypeStruct(dims, kind)


def one_hot_rows(col, count):
    tiles = [col == iota((LANES, LANES), 1) + LANES * j for j in range(count // LANES)]
    return jnp.concatenate([t.astype(F32).astype(BF16) for t in tiles], axis=1)


def one_hot_columns(row, count):
    return (iota((count, LANES), 0) == row).astype(F32).astype(BF16)


def unfold(wide, high):
    out = jnp.where(high == 0, wide[:, :LANES], 0.0)
    for j in range(1, FOLD):
        out = jnp.where(high == j, wide[:, j * LANES : (j + 1) * LANES], out)
    return out


def fold(rows, high):
    return jnp.concatenate(
        [jnp.where(high == j, rows, 0.0).astype(BF16) for j in range(FOLD)], axis=1
    )


def place_body(wanted_ref, slots_ref, ids_ref):
    blocks = REQ // LANES
    earlier = (iota((REQ, REQ), 0) < iota((REQ, REQ), 1)).astype(F32).astype(BF16)
    high_sum = jnp.zeros((OWNERS, LANES), F32)
    low_sum = jnp.zeros((OWNERS, LANES), F32)
    for g in range(2):
        owner_hits = []
        for b in range(blocks):
            row = wanted_ref[g, b : b + 1, :]
            owner_hits.append(iota((OWNERS, LANES), 0) == (row >> 11))
        hits = jnp.concatenate([h.astype(F32).astype(BF16) for h in owner_hits], axis=1)
        before = dot(hits, earlier)
        for b in range(blocks):
            row = wanted_ref[g, b : b + 1, :]
            mine = before[:, b * LANES : (b + 1) * LANES]
            rank = jnp.sum(jnp.where(owner_hits[b], mine, 0.0), axis=0, keepdims=True)
            rank = rank.astype(I32)
            slots_ref[g, b : b + 1, :] = (row >> 11) * CAP + rank
            value = (row & 2047) + 1
            at = column(rank) + CAP * g == iota((LANES, LANES), 1)
            val = column(value)
            hit = hits[:, b * LANES : (b + 1) * LANES]
            high_sum += dot(hit, jnp.where(at, (val >> 6).astype(F32), 0.0).astype(BF16))
            low_sum += dot(hit, jnp.where(at, (val & 63).astype(F32), 0.0).astype(BF16))
    ids_ref[...] = (high_sum * 64.0 + low_sum).astype(I32)


def place(wanted):
    outs = (shape((2, REQ // LANES, LANES), I32), shape((OWNERS, LANES), I32))
    return kernel_call(place_body, outs, name="place", flops=1 << 27)(wanted)


def look_up_body(ids_ref, table_ref, out_ref, folded):
    for j in range(FOLD):
        folded[:, j * LANES : (j + 1) * LANES] = table_ref[
            j * SPLIT : (j + 1) * SPLIT, :
        ].astype(BF16)

    def step(i, _):
        at = column(ids_ref[pl.ds(i, 1), :]) - 1
        low = jnp.where(at >= 0, at & (SPLIT - 1), -1)
        wide = dot(one_hot_rows(low, SPLIT), folded[...])
        out_ref[i] = unfold(wide, at >> 9).astype(BF16)
        return 0

    lax.fori_loop(0, OWNERS, step, 0, unroll=4)


def look_up(ids, table):
    return kernel_call(
        look_up_body,
        shape((OWNERS, LANES, LANES), BF16),
        scratch=[pltpu.VMEM((SPLIT, FOLD * LANES), BF16)],
        name="look_up",
        flops=1 << 31,
    )(ids, table)


def score_body(g_ref, arrived_ref, slots_ref, rel_ref, rows_ref, query_ref, probe_ref, out_ref, wide):
    g = g_ref[0]
    for j in range(FOLD):
        part = arrived_ref[j * 8 : (j + 1) * 8, pl.ds(pl.multiple_of(g * CAP, CAP), CAP), :]
        wide[:, j * LANES : (j + 1) * LANES] = part.reshape(SPLIT, LANES)
    for b in range(REQ // LANES):
        at = column(slots_ref[g, b : b + 1, :])
        picked = dot(one_hot_rows(at & (SPLIT - 1), SPLIT), wide[...])
        rows_ref[b * LANES : (b + 1) * LANES, :] = unfold(picked, at >> 9).astype(BF16)
    head = rows_ref[:GROUP, :].astype(F32)
    tail = rows_ref[GROUP : 2 * GROUP, :].astype(F32)
    noise = rows_ref[2 * GROUP :, :]
    rel = rel_ref[g].astype(BF16).astype(F32)
    query = product(head, rel).astype(BF16)
    probe = product(tail, rel, -1.0).astype(BF16)
    query_ref[...] = query
    probe_ref[...] = probe
    pos = jnp.sum(jnp.transpose(query.astype(F32) * tail), axis=0, keepdims=True)
    for side, left in enumerate((query, probe)):
        both = dot(left, noise, ((1,), (1,))).astype(BF16)
        for q in range(4):
            for c in range(2):
                out_ref[q, (2 * side + c) * 64 : (2 * side + c + 1) * 64, :] = both[
                    q * 64 : (q + 1) * 64, c * LANES : (c + 1) * LANES
                ]
    for q in range(4):
        row = pos[:, (q // 2) * LANES : (q // 2 + 1) * LANES]
        out_ref[q, 256:PART, :] = jnp.broadcast_to(row, (PART - 256, LANES)).astype(BF16)


def score(g, arrived, slots, rel):
    outs = (
        shape((REQ, LANES), BF16),
        shape((GROUP, LANES), BF16),
        shape((GROUP, LANES), BF16),
        shape((4, PART, LANES), BF16),
    )
    return kernel_call(
        score_body,
        outs,
        n_smem=1,
        scratch=[pltpu.VMEM((SPLIT, FOLD * LANES), BF16)],
        name="score",
        flops=1 << 29,
    )(g, arrived, slots, rel)


def add_body(x_ref, kept_ref, other_ref, *out_refs):
    x = x_ref[0]
    for s in range(4):
        q = lax.rem(x + s, 4)
        out_refs[s][...] = (kept_ref[q].astype(F32) + other_ref[q].astype(F32)).astype(BF16)


def add_and_turn(x, kept, other):
    outs = tuple(shape((PART, LANES), BF16) for _ in range(4))
    return kernel_call(add_body, outs, n_smem=1, name="add_and_turn")(x, kept, other)


def coef_body(a_ref, b_ref, c_ref, d_ref, out_ref):
    total = (a_ref[...].astype(F32) + b_ref[...].astype(F32)) + (
        c_ref[...].astype(F32) + d_ref[...].astype(F32)
    )
    out_ref[:256, :] = (jax.nn.sigmoid(total[:256, :]) / NEG).astype(BF16)
    out_ref[256:, :] = (-jax.nn.sigmoid(-total[256:, :])).astype(BF16)


def coefficients(*parts):
    return kernel_call(coef_body, shape((PART, LANES), BF16), name="coefficients")(*parts)


def grad_body(
    x_ref, g_ref, coef_ref, rows_ref, query_ref, probe_ref, rel_ref, slots_ref,
    out_ref, relrow_ref, tail_c, head_c, pos_s, wide, hot,
):
    x = x_ref[0]
    g = g_ref[0]
    for s in range(4):
        q = lax.rem(x + 4 - s, 4)
        at = pl.ds(pl.multiple_of(q * 64, 64), 64)
        for c in range(2):
            lanes = slice(c * LANES, (c + 1) * LANES)
            tail_c[at, lanes] = coef_ref[s, c * 64 : (c + 1) * 64, :]
            head_c[at, lanes] = coef_ref[s, (2 + c) * 64 : (3 + c) * 64, :]
        pos_s[q] = coef_ref[s, 256:PART, :].astype(F32)
    pos = jnp.concatenate([column(pos_s[0, :1, :]), column(pos_s[2, :1, :])], axis=0)
    head = rows_ref[:GROUP, :].astype(F32)
    tail = rows_ref[GROUP : 2 * GROUP, :].astype(F32)
    noise = rows_ref[2 * GROUP :, :]
    rel = rel_ref[g].astype(BF16).astype(F32)
    tail_pull = pos * tail + dot(tail_c[...], noise)
    head_pull = dot(head_c[...], noise)
    head_side = pos * head + head_pull
    head_grad = product(tail_pull, rel, -1.0)
    tail_grad = product(head_side, rel)
    noise_grad = dot(tail_c[...], query_ref[...], ((0,), (0,))) + dot(
        head_c[...], probe_ref[...], ((0,), (0,))
    )
    relrow_ref[...] = (
        product(tail_pull, head, -1.0) + product(tail, head_pull, -1.0)
    ).astype(BF16)
    for b in range(REQ // LANES):
        part = (head_grad, tail_grad, noise_grad)[b // 2][(b % 2) * LANES : (b % 2 + 1) * LANES]
        row = slots_ref[g, b : b + 1, :]
        wide[b * LANES : (b + 1) * LANES, :] = fold(part, column(row) >> 9)
        hot[:, b * LANES : (b + 1) * LANES] = one_hot_columns(row & (SPLIT - 1), SPLIT)
    packed = dot(hot[...], wide[...])
    for j in range(FOLD):
        out_ref[j * 8 : (j + 1) * 8] = (
            packed[:, j * LANES : (j + 1) * LANES].astype(BF16).reshape(8, CAP, LANES)
        )


def gradients(x, g, coef, rows, query, probe, rel, slots):
    outs = (shape((OWNERS, CAP, LANES), BF16), shape((GROUP, LANES), BF16))
    return kernel_call(
        grad_body,
        outs,
        n_smem=2,
        scratch=[
            pltpu.VMEM((GROUP, NEG), BF16),
            pltpu.VMEM((GROUP, NEG), BF16),
            pltpu.VMEM((4, PART - 256, LANES), F32),
            pltpu.VMEM((REQ, FOLD * LANES), BF16),
            pltpu.VMEM((SPLIT, REQ), BF16),
        ],
        name="gradients",
        flops=1 << 30,
    )(x, g, coef, rows, query, probe, rel, slots)


def accumulate_body(ids_ref, back_ref, reg_ref, total_ref, square_ref, wide, hot):
    def step(i, _):
        row = ids_ref[pl.ds(i, 1), :] - 1
        low = jnp.where(row >= 0, row & (SPLIT - 1), -1)
        at = pl.ds(pl.multiple_of(i * LANES, LANES), LANES)
        wide[at, :] = fold(back_ref[i].astype(F32), column(row) >> 9)
        hot[:, at] = one_hot_columns(low, SPLIT)
        return 0

    lax.fori_loop(0, OWNERS, step, 0, unroll=4)
    for m in range(SPLIT // LANES):
        packed = dot(hot[m * LANES : (m + 1) * LANES, :], wide[...])
        for j in range(FOLD):
            at = slice(j * SPLIT + m * LANES, j * SPLIT + (m + 1) * LANES)
            total = packed[:, j * LANES : (j + 1) * LANES] + reg_ref[at, :]
            total_ref[at, :] = total
            row = j * FOLD + m
            square_ref[row : row + 1, :] = jnp.sum(
                jnp.transpose(total * total), axis=0, keepdims=True
            )


def accumulate(ids, back, reg):
    rows = FOLD * SPLIT
    return kernel_call(
        accumulate_body,
        (shape((rows, LANES), F32), shape((rows // LANES, LANES), F32)),
        scratch=[
            pltpu.VMEM((OWNERS * LANES, FOLD * LANES), BF16),
            pltpu.VMEM((SPLIT, OWNERS * LANES), BF16),
        ],
        name="accumulate",
        flops=1 << 31,
    )(ids, back, reg)


def step_body(table_ref, total_ref, state_ref, square_ref, out_ref):
    for b in range(table_ref.shape[0] // LANES):
        at = slice(b * LANES, (b + 1) * LANES)
        root = lax.sqrt(state_ref[b : b + 1, :] + square_ref[b : b + 1, :] / (2 * RANK))
        scale = column(LEARN_RATE / root)
        out_ref[at, :] = table_ref[at, :] - total_ref[at, :] * scale


def entity_step(table, total, state, square):
    return kernel_call(step_body, shape(table.shape, F32), name="entity_step")(
        table, total, state, square
    )


def rel_sum_body(e_ref, *refs):
    ids, rows = refs[:4], refs[4:8]
    outs, wide, hot, total = refs[8:16], refs[16], refs[17], refs[18]
    y = e_ref[0] >> 3
    z = e_ref[0] & 7
    for s in range(4):
        for b in range(4):
            row = ids[s][b : b + 1, :] - y * 1024
            inside = (row >= 0) & (row < 1024)
            low = jnp.where(inside, row & 255, -1)
            at = slice(s * 512 + b * LANES, s * 512 + (b + 1) * LANES)
            wide[at, :] = fold(rows[s][b * LANES : (b + 1) * LANES, :].astype(F32), column(row) >> 8)
            hot[:, at] = one_hot_columns(low, 256)
    packed = dot(hot[...], wide[...]).astype(BF16)
    for k in range(8):
        total[k] = packed[(k % 2) * LANES : (k % 2 + 1) * LANES, (k // 2) * LANES : (k // 2 + 1) * LANES]
    for s in range(8):
        outs[s][...] = total[(z + s) & 7]


def rel_sum(e, ids, rows):
    outs = tuple(shape((LANES, LANES), BF16) for _ in range(8))
    return kernel_call(
        rel_sum_body,
        outs,
        n_smem=1,
        scratch=[
            pltpu.VMEM((2048, FOLD * LANES), BF16),
            pltpu.VMEM((256, 2048), BF16),
            pltpu.VMEM((8, LANES, LANES), BF16),
        ],
        name="rel_sum",
        flops=1 << 29,
    )(e, *ids, *rows)


def rel_total_body(*refs):
    total = refs[0][...].astype(F32)
    for ref in refs[1:8]:
        total += ref[...].astype(F32)
    refs[8][...] = total
    square = jnp.sum(jnp.transpose(total * total), axis=0, keepdims=True)
    refs[9][...] = jnp.broadcast_to(square, (8, LANES))


def rel_total(parts):
    outs = (shape((LANES, LANES), F32), shape((8, LANES), F32))
    return kernel_call(rel_total_body, outs, name="rel_total")(*parts)


def rel_update_body(e_ref, total_ref, square_ref, state_ref, out_ref):
    state = state_ref[pl.ds(e_ref[0], 1), :]
    root = lax.sqrt(state + square_ref[:1, :] / (2 * RANK))
    out_ref[...] = (total_ref[...] * column(LEARN_RATE / root)).astype(BF16)


def rel_update(e, total, square, state):
    return kernel_call(rel_update_body, shape((LANES, LANES), BF16), n_smem=1, name="rel_update")(
        e, total, square, state
    )


def rel_join_body(e_ref, *refs):
    z = e_ref[0] & 7
    for s in range(8):
        refs[8][(z + 8 - s) & 7] = refs[s][...]


def rel_join(e, parts):
    return kernel_call(rel_join_body, shape((8, LANES, LANES), BF16), n_smem=1, name="rel_join")(
        e, *parts
    )


def rel_step_body(e_ref, table_ref, *refs):
    y = e_ref[0] >> 3
    for s in range(4):
        at = pl.ds(pl.multiple_of(((y + 4 - s) & 3) * 1024, 1024), 1024)
        refs[4][at, :] = table_ref[at, :] - refs[s][...].astype(F32)


def rel_step(e, table, parts):
    return kernel_call(rel_step_body, shape(table.shape, F32), n_smem=1, name="rel_step")(
        e, table, *parts
    )


def y_turn(s):
    return [(y * Z + z, (y + s) % Y * Z + z) for y in range(Y) for z in range(Z)]


def z_turn(s):
    return [(y * Z + z, y * Z + (z + s) % Z) for y in range(Y) for z in range(Z)]


def x_turn(s):
    return [(x * 2 + c, (x + s) % X * 2 + c) for x in range(X) for c in range(2)]


def flip(bit):
    return [(i, i ^ bit) for i in range(X * CORES)]


def around(array, axis, turn, count):
    return [array] + [lax.ppermute(array, axis, turn(s)) for s in range(1, count)]


def scattered(parts, axis, turn):
    return [parts[0]] + [lax.ppermute(p, axis, turn(s)) for s, p in enumerate(parts) if s]


def summed_over_dim(values):
    for bit in (1, 2, 4):
        values = values + lax.ppermute(values, "dim", flip(bit))
    return values


def per_device(entities, ent_state, buckets, relations, rel_state, triples, negatives):
    rows_here = entities.shape[0]
    e = lax.axis_index("ent").reshape(1)
    d = lax.axis_index("dim")
    x = (d >> 1).reshape(1)
    mine = (d & 1).reshape(1)
    other = 1 - mine
    triple_ids = triples.reshape(3, 2, 2, LANES)
    wanted = jnp.concatenate(
        [triple_ids[0], triple_ids[2], negatives.reshape(2, 2, LANES)], axis=1
    )
    slots, out_ids = place(wanted)
    ids = lax.all_to_all(out_ids, "ent", 0, 0, tiled=True)
    arrived = lax.all_to_all(look_up(ids, entities), "ent", 0, 0, tiled=True)
    rel_ids = triples[1].reshape(4, LANES)
    near_ids = around(rel_ids, "ent", y_turn, Y)
    rel = jnp.take(relations, triples[1], axis=0, mode="clip").reshape(2, GROUP, LANES)
    flat = ids.reshape(-1) - 1
    counts = jnp.sum(
        (flat[:, None] == jnp.arange(rows_here, dtype=I32)[None, :]).astype(F32), axis=0
    )
    weight = REG_WEIGHT * (buckets.astype(F32) + 1.0) * counts
    reg = weight[:, None] * 3.0 * entities * jnp.abs(entities)

    sent = score(other, arrived, slots, rel)
    swapped = lax.ppermute(sent[3], "dim", flip(1))
    kept = score(mine, arrived, slots, rel)
    parts = scattered(add_and_turn(x, kept[3], swapped), "dim", x_turn)
    coef = jnp.stack(around(coefficients(*parts), "dim", x_turn, X))
    coef_other = lax.ppermute(coef, "dim", flip(1))
    my_pack, my_rel = gradients(x, mine, coef, kept[0], kept[1], kept[2], rel, slots)
    other_pack, other_rel = gradients(x, other, coef_other, sent[0], sent[1], sent[2], rel, slots)
    first = (mine == 0)[0]
    rel_rows = jnp.where(
        first,
        jnp.concatenate([my_rel, other_rel], axis=0),
        jnp.concatenate([other_rel, my_rel], axis=0),
    )
    packed = jnp.where(
        first,
        jnp.concatenate([my_pack, other_pack], axis=1),
        jnp.concatenate([other_pack, my_pack], axis=1),
    )
    near_rows = around(rel_rows, "ent", y_turn, Y)
    returned = lax.all_to_all(packed, "ent", 0, 0, tiled=True)
    parts = scattered(rel_sum(e, near_ids, near_rows), "ent", z_turn)
    total, square = rel_total(parts)
    square = summed_over_dim(square)
    update = rel_update(e, total, square, rel_state.reshape(OWNERS, LANES))
    joined = rel_join(e, around(update, "ent", z_turn, Z)).reshape(1024, LANES)
    new_relations = rel_step(e, relations, around(joined, "ent", y_turn, Y))

    ent_total, ent_square = accumulate(ids, returned, reg)
    ent_square = summed_over_dim(ent_square)
    new_entities = entity_step(
        entities, ent_total, ent_state.reshape(rows_here // LANES, LANES), ent_square
    )
    return (new_entities, new_relations)


def solution(mesh):
    placed = (
        P("ent", "dim"),
        P("ent"),
        P("ent"),
        P(None, "dim"),
        P(),
        P(None, "ent"),
        P("ent", None),
    )
    return jax.shard_map(
        per_device,
        mesh=mesh,
        in_specs=placed,
        out_specs=(P("ent", "dim"), P(None, "dim")),
        check_vma=False,
    )
```

```python
import functools

import jax
import jax.numpy as jnp
from jax import lax
from jax.experimental import pallas as pl
from jax.experimental.pallas import tpu as pltpu
from jax.sharding import PartitionSpec as P

RANK = 512
HALF = 64
LANES = 128
LEARN_RATE = 0.1
REG_WEIGHT = 0.01
Y, Z, X, CORES = 4, 8, 4, 2
OWNERS = Y * Z
GROUP = 256
NEG = 256
REQ = 768
CAP = 64
SPLIT = 512
FOLD = 4
PART = 272
F32, BF16, I32 = jnp.float32, jnp.bfloat16, jnp.int32


VMEM = pl.BlockSpec(memory_space=pltpu.VMEM)
SMEM = pl.BlockSpec(memory_space=pltpu.SMEM)
HBM = pl.BlockSpec(memory_space=pltpu.HBM)


def iota(shape, dim):
    return lax.broadcasted_iota(I32, shape, dim)


def column(row):
    return jnp.transpose(jnp.broadcast_to(row, (LANES, LANES)))


def swap(values):
    return pltpu.roll(values, HALF, 1)


def low_half(shape):
    return iota(shape, 1) < HALF


def product(former, latter, sign=1.0):
    low = low_half(former.shape)
    turned = swap(latter)
    real = jnp.where(low, latter, turned)
    imag = jnp.where(low, -sign * turned, sign * latter)
    return former * real + swap(former) * imag


def dot(a, b, dims=((1,), (0,))):
    return lax.dot_general(a, b, (dims, ((), ())), preferred_element_type=F32)


def kernel_call(body, outs, ins, scratch=(), name=None, flops=0, limit=12, out_specs=None):
    out_specs = out_specs or jax.tree.map(lambda _: VMEM, outs)
    outs = jax.tree.map(
        lambda o, spec: pltpu.HBM(o.shape, o.dtype) if spec is HBM else o, outs, out_specs
    )

    def call(*args):
        args = [
            pltpu.with_memory_space_constraint(a, pltpu.HBM) if spec is HBM else a
            for a, spec in zip(args, ins)
        ]
        return pl.pallas_call(
            body,
            out_shape=outs,
            in_specs=list(ins),
            out_specs=out_specs,
            scratch_shapes=list(scratch),
            name=name,
            compiler_params=pltpu.CompilerParams(vmem_limit_bytes=limit << 20),
            cost_estimate=pl.CostEstimate(
                flops=flops,
                transcendentals=0,
                bytes_accessed=sum(a.size * a.dtype.itemsize for a in args),
            ),
        )(*args)

    return call


def started(source, target, sem):
    copy = pltpu.make_async_copy(source, target, sem)
    copy.start()
    return copy


def shape(dims, kind):
    return jax.ShapeDtypeStruct(dims, kind)


def one_hot_rows(col, count):
    tiles = [col == iota((LANES, LANES), 1) + LANES * j for j in range(count // LANES)]
    return jnp.concatenate([t.astype(F32).astype(BF16) for t in tiles], axis=1)


def one_hot_columns(row, count):
    return (iota((count, LANES), 0) == row).astype(F32).astype(BF16)


def unfold(wide, high):
    out = jnp.where(high == 0, wide[:, :LANES], 0.0)
    for j in range(1, FOLD):
        out = jnp.where(high == j, wide[:, j * LANES : (j + 1) * LANES], out)
    return out


def fold(rows, high):
    return jnp.concatenate(
        [jnp.where(high == j, rows, 0.0).astype(BF16) for j in range(FOLD)], axis=1
    )


def place_body(
    core_ref, triples_hbm, negatives_hbm, slots_ref, ids_ref, rel_ref, triples_ref, negatives_ref, sems
):
    copies = [
        started(triples_hbm, triples_ref, sems.at[0]),
        started(negatives_hbm, negatives_ref, sems.at[1]),
    ]
    blocks = REQ // LANES
    earlier = (iota((REQ, REQ), 0) < iota((REQ, REQ), 1)).astype(F32).astype(BF16)
    high_sum = jnp.zeros((OWNERS, LANES), F32)
    low_sum = jnp.zeros((OWNERS, LANES), F32)
    for copy in copies:
        copy.wait()
    for k in range(2):
        flip_groups = core_ref[0] != k

        def pick(ref, row, block, step):
            first = ref[row[0] : row[0] + 1, block * LANES : (block + 1) * LANES]
            block += step
            second = ref[row[1] : row[1] + 1, block * LANES : (block + 1) * LANES]
            return jnp.where(flip_groups, second, first)

        for c in range(2):
            rel_ref[2 * k + c : 2 * k + c + 1, :] = pick(triples_ref, (1, 1), c, 2)
        rows = [pick(triples_ref, (kind, kind), c, 2) for kind in (0, 2) for c in range(2)]
        rows += [pick(negatives_ref, (0, 1), c, 0) for c in range(2)]
        owner_hits = [iota((OWNERS, LANES), 0) == (row >> 11) for row in rows]
        hits = jnp.concatenate([h.astype(F32).astype(BF16) for h in owner_hits], axis=1)
        before = dot(hits, earlier)
        for b in range(blocks):
            row = rows[b]
            mine = before[:, b * LANES : (b + 1) * LANES]
            rank = jnp.sum(jnp.where(owner_hits[b], mine, 0.0), axis=0, keepdims=True)
            rank = rank.astype(I32)
            slots_ref[k, b : b + 1, :] = (row >> 11) * CAP + rank
            value = (row & 2047) + 1
            at = column(rank) + CAP * k == iota((LANES, LANES), 1)
            val = column(value)
            hit = hits[:, b * LANES : (b + 1) * LANES]
            high_sum += dot(hit, jnp.where(at, (val >> 6).astype(F32), 0.0).astype(BF16))
            low_sum += dot(hit, jnp.where(at, (val & 63).astype(F32), 0.0).astype(BF16))
    ids_ref[...] = (high_sum * 64.0 + low_sum).astype(I32)


def place(core, triples, negatives):
    outs = (
        shape((2, REQ // LANES, LANES), I32),
        shape((OWNERS, LANES), I32),
        shape((4, LANES), I32),
    )
    return kernel_call(
        place_body,
        outs,
        (SMEM, HBM, HBM),
        scratch=[
            pltpu.VMEM(triples.shape, I32),
            pltpu.VMEM(negatives.shape, I32),
            pltpu.SemaphoreType.DMA((2,)),
        ],
        name="place",
        flops=1 << 27,
    )(core, triples, negatives)


def fold_body(table_hbm, out_hbm, table_ref, out_ref, sems):
    copies = [
        started(
            table_hbm.at[j * SPLIT : (j + 1) * SPLIT],
            table_ref.at[j * SPLIT : (j + 1) * SPLIT],
            sems.at[j],
        )
        for j in range(FOLD)
    ]
    for j in range(FOLD):
        copies[j].wait()
        out_ref[:, j * LANES : (j + 1) * LANES] = table_ref[
            j * SPLIT : (j + 1) * SPLIT, :
        ].astype(BF16)
    started(out_ref, out_hbm, sems.at[FOLD]).wait()


def fold_table(table):
    return kernel_call(
        fold_body,
        shape((SPLIT, FOLD * LANES), BF16),
        (HBM,),
        scratch=[
            pltpu.VMEM(table.shape, F32),
            pltpu.VMEM((SPLIT, FOLD * LANES), BF16),
            pltpu.SemaphoreType.DMA((FOLD + 1,)),
        ],
        out_specs=HBM,
        name="fold_table",
        flops=1 << 22,
    )(table)


def look_up_body(ids_ref, table_hbm, out_hbm, table_ref, rows, sems):
    started(table_hbm, table_ref, sems.at[OWNERS // 8]).wait()

    def leave(k):
        at = pl.ds(k * 8, 8)
        return pltpu.make_async_copy(rows.at[at], out_hbm.at[at], sems.at[k])

    def step(k, _):
        ids = ids_ref[pl.ds(pl.multiple_of(k * 8, 8), 8), :]
        for i in range(8):
            at = column(ids[i : i + 1, :]) - 1
            low = jnp.where(at >= 0, at & (SPLIT - 1), -1)
            wide = dot(one_hot_rows(low, SPLIT), table_ref[...])
            rows[k * 8 + i] = unfold(wide, at >> 9).astype(BF16)
        leave(k).start()
        return 0

    lax.fori_loop(0, OWNERS // 8, step, 0)
    for k in range(OWNERS // 8):
        leave(k).wait()


def look_up(ids, table):
    return kernel_call(
        look_up_body,
        shape((OWNERS, LANES, LANES), BF16),
        (VMEM, HBM),
        scratch=[
            pltpu.VMEM((SPLIT, FOLD * LANES), BF16),
            pltpu.VMEM((OWNERS, LANES, LANES), BF16),
            pltpu.SemaphoreType.DMA((OWNERS // 8 + 1,)),
        ],
        out_specs=HBM,
        name="look_up",
        flops=1 << 31,
    )(ids, table)


def spread_body(ids_ref, out_hbm, out_ref, sem):
    for i in range(OWNERS):
        row = ids_ref[i : i + 1, :] - 1
        low = jnp.where(row >= 0, row & (SPLIT - 1), -1)
        out_ref[:, i * LANES : (i + 1) * LANES] = one_hot_columns(low, SPLIT)
    started(out_ref, out_hbm, sem).wait()


def spread(ids):
    pairs = OWNERS * LANES
    return kernel_call(
        spread_body,
        shape((SPLIT, pairs), BF16),
        (VMEM,),
        scratch=[pltpu.VMEM((SPLIT, pairs), BF16), pltpu.SemaphoreType.DMA],
        out_specs=HBM,
        name="spread",
        flops=1 << 22,
    )(ids)


def score_body(
    g, arrived_hbm, slots_ref, rel_ref, rows_ref, query_ref, probe_ref, out_ref, wide, sems
):
    copies = [
        started(
            arrived_hbm.at[j * 8 : (j + 1) * 8, g * CAP : (g + 1) * CAP, :],
            wide.at[:, :, j * LANES : (j + 1) * LANES],
            sems.at[j],
        )
        for j in range(FOLD)
    ]
    for copy in copies:
        copy.wait()
    table = wide[...].reshape(SPLIT, FOLD * LANES)
    for b in range(REQ // LANES):
        at = column(slots_ref[g, b : b + 1, :])
        picked = dot(one_hot_rows(at & (SPLIT - 1), SPLIT), table)
        rows_ref[b * LANES : (b + 1) * LANES, :] = unfold(picked, at >> 9).astype(BF16)
    head = rows_ref[:GROUP, :].astype(F32)
    tail = rows_ref[GROUP : 2 * GROUP, :].astype(F32)
    noise = rows_ref[2 * GROUP :, :]
    rel = rel_ref[g].astype(BF16).astype(F32)
    query = product(head, rel).astype(BF16)
    probe = product(tail, rel, -1.0).astype(BF16)
    query_ref[...] = query
    probe_ref[...] = probe
    pos = jnp.sum(jnp.transpose(query.astype(F32) * tail), axis=0, keepdims=True)
    for side, left in enumerate((query, probe)):
        both = dot(left, noise, ((1,), (1,))).astype(BF16)
        for q in range(4):
            for c in range(2):
                out_ref[q, (2 * side + c) * 64 : (2 * side + c + 1) * 64, :] = both[
                    q * 64 : (q + 1) * 64, c * LANES : (c + 1) * LANES
                ]
    for q in range(4):
        row = pos[:, (q // 2) * LANES : (q // 2 + 1) * LANES]
        out_ref[q, 256:PART, :] = jnp.broadcast_to(row, (PART - 256, LANES)).astype(BF16)


def score(g, arrived, slots, rel):
    outs = (
        shape((REQ, LANES), BF16),
        shape((GROUP, LANES), BF16),
        shape((GROUP, LANES), BF16),
        shape((4, PART, LANES), BF16),
    )
    return kernel_call(
        functools.partial(score_body, g),
        outs,
        (HBM, VMEM, VMEM),
        scratch=[
            pltpu.VMEM((8, CAP, FOLD * LANES), BF16),
            pltpu.SemaphoreType.DMA((FOLD,)),
        ],
        name="score",
        flops=1 << 29,
    )(arrived, slots, rel)


def add_body(kept_ref, other_ref, out_ref):
    out_ref[...] = (kept_ref[...].astype(F32) + other_ref[...].astype(F32)).astype(BF16)


def added(kept, other):
    return kernel_call(add_body, shape(kept.shape, BF16), (VMEM, VMEM), name="added")(kept, other)


def coef_body(a_ref, b_ref, out_ref):
    for q in range(4):
        total = a_ref[q].astype(F32) + b_ref[q].astype(F32)
        out_ref[q, :256, :] = (jax.nn.sigmoid(total[:256, :]) / NEG).astype(BF16)
        out_ref[q, 256:, :] = (-jax.nn.sigmoid(-total[256:, :])).astype(BF16)


def coefficients(a, b):
    return kernel_call(
        coef_body, shape((4, PART, LANES), BF16), (VMEM, VMEM), name="coefficients"
    )(a, b)


def grad_body(mine_ref, other_ref, rows0, query0, probe0, rows1, query1, probe1, *refs):
    rel_ref, slots_ref, out_hbm, relrow_ref, out_ref, tail_c, head_c, wide, hot, sems = refs
    copies = []
    groups = ((mine_ref, rows0, query0, probe0), (other_ref, rows1, query1, probe1))
    for g, (coef_ref, rows_ref, query_ref, probe_ref) in enumerate(groups):
        for q in range(4):
            at = slice(q * 64, (q + 1) * 64)
            for c in range(2):
                lanes = slice(c * LANES, (c + 1) * LANES)
                tail_c[at, lanes] = coef_ref[q, c * 64 : (c + 1) * 64, :]
                head_c[at, lanes] = coef_ref[q, (2 + c) * 64 : (3 + c) * 64, :]
        pos = [column(coef_ref[q, 256:PART, :].astype(F32)[:1, :]) for q in (0, 2)]
        pos = jnp.concatenate(pos, axis=0)
        head = rows_ref[:GROUP, :].astype(F32)
        tail = rows_ref[GROUP : 2 * GROUP, :].astype(F32)
        noise = rows_ref[2 * GROUP :, :]
        rel = rel_ref[g].astype(BF16).astype(F32)
        tail_pull = pos * tail + dot(tail_c[...], noise)
        head_pull = dot(head_c[...], noise)
        head_side = pos * head + head_pull
        head_grad = product(tail_pull, rel, -1.0)
        tail_grad = product(head_side, rel)
        noise_grad = dot(tail_c[...], query_ref[...], ((0,), (0,))) + dot(
            head_c[...], probe_ref[...], ((0,), (0,))
        )
        relrow_ref[g * GROUP : (g + 1) * GROUP, :] = (
            product(tail_pull, head, -1.0) + product(tail, head_pull, -1.0)
        ).astype(BF16)
        for b in range(REQ // LANES):
            at = slice((b % 2) * LANES, (b % 2 + 1) * LANES)
            part = (head_grad, tail_grad, noise_grad)[b // 2][at]
            row = slots_ref[g, b : b + 1, :]
            at = slice(b * LANES, (b + 1) * LANES)
            wide[at, :] = fold(part, column(row) >> 9)
            hot[:, at] = one_hot_columns(row & (SPLIT - 1), SPLIT)
        for k in range(SPLIT // LANES):
            packed = dot(hot[k * LANES : (k + 1) * LANES, :], wide[...])
            for j in range(FOLD):
                piece = packed[:, j * LANES : (j + 1) * LANES].astype(BF16)
                first = j * 8 + k * 2
                out_ref[g, first : first + 2] = piece.reshape(2, CAP, LANES)
        copies.append(started(out_ref.at[g], out_hbm.at[:, g * CAP : (g + 1) * CAP, :], sems.at[g]))
    for copy in copies:
        copy.wait()


def gradients(mine, other, kept, sent, rel, slots):
    outs = (shape((OWNERS, 2 * CAP, LANES), BF16), shape((2 * GROUP, LANES), BF16))
    return kernel_call(
        grad_body,
        outs,
        (VMEM,) * 10,
        scratch=[
            pltpu.VMEM((2, OWNERS, CAP, LANES), BF16),
            pltpu.VMEM((GROUP, NEG), BF16),
            pltpu.VMEM((GROUP, NEG), BF16),
            pltpu.VMEM((REQ, FOLD * LANES), BF16),
            pltpu.VMEM((SPLIT, REQ), BF16),
            pltpu.SemaphoreType.DMA((2,)),
        ],
        out_specs=(HBM, VMEM),
        name="gradients",
        flops=1 << 30,
    )(mine, other, *kept, *sent, rel, slots)


def accumulate_body(
    ids_ref, back_hbm, reg_hbm, hot_hbm, total_ref, square_ref, back_ref, reg_ref, hot, wide, sems
):
    pieces = 4
    step = OWNERS // pieces
    backs = [
        started(
            back_hbm.at[k * step : (k + 1) * step], back_ref.at[k * step : (k + 1) * step], sems.at[k]
        )
        for k in range(pieces)
    ]
    hot_copy = started(hot_hbm, hot, sems.at[pieces])
    reg_copy = started(reg_hbm, reg_ref, sems.at[pieces + 1])
    for k in range(pieces):
        backs[k].wait()
        for i in range(k * step, (k + 1) * step):
            row = ids_ref[i : i + 1, :] - 1
            wide[i * LANES : (i + 1) * LANES, :] = fold(
                back_ref[i].astype(F32), column(row) >> 9
            )
    hot_copy.wait()
    reg_copy.wait()
    for m in range(SPLIT // LANES):
        packed = dot(hot[m * LANES : (m + 1) * LANES, :], wide[...])
        for j in range(FOLD):
            at = slice(j * SPLIT + m * LANES, j * SPLIT + (m + 1) * LANES)
            total = packed[:, j * LANES : (j + 1) * LANES] + reg_ref[at, :]
            total_ref[at, :] = total
            row = j * FOLD + m
            square_ref[row : row + 1, :] = jnp.sum(
                jnp.transpose(total * total), axis=0, keepdims=True
            )


def accumulate(ids, back, reg, hot):
    rows = FOLD * SPLIT
    pairs = OWNERS * LANES
    return kernel_call(
        accumulate_body,
        (shape((rows, LANES), F32), shape((rows // LANES, LANES), F32)),
        (VMEM, HBM, HBM, HBM),
        scratch=[
            pltpu.VMEM((OWNERS, LANES, LANES), BF16),
            pltpu.VMEM((rows, LANES), F32),
            pltpu.VMEM((SPLIT, pairs), BF16),
            pltpu.VMEM((pairs, FOLD * LANES), BF16),
            pltpu.SemaphoreType.DMA((6,)),
        ],
        name="accumulate",
        flops=1 << 31,
        limit=24,
    )(ids, back, reg, hot)


def step_body(table_ref, total_ref, state_ref, square_ref, out_ref):
    for b in range(table_ref.shape[0] // LANES):
        at = slice(b * LANES, (b + 1) * LANES)
        root = lax.sqrt(state_ref[b : b + 1, :] + square_ref[b : b + 1, :] / (2 * RANK))
        scale = column(LEARN_RATE / root)
        out_ref[at, :] = table_ref[at, :] - total_ref[at, :] * scale


def entity_step(table, total, state, square):
    return kernel_call(step_body, shape(table.shape, F32), (VMEM,) * 4, name="entity_step")(
        table, total, state, square
    )


def rel_sum_body(e_ref, *refs):
    ids, rows = refs[:4], refs[4:8]
    out_ref, wide, hot = refs[8:]
    y = e_ref[0] >> 3
    for s in range(4):
        for b in range(4):
            row = ids[s][b : b + 1, :] - y * 1024
            inside = (row >= 0) & (row < 1024)
            low = jnp.where(inside, row & 255, -1)
            at = slice(s * 512 + b * LANES, s * 512 + (b + 1) * LANES)
            wide[at, :] = fold(rows[s][b * LANES : (b + 1) * LANES, :].astype(F32), column(row) >> 8)
            hot[:, at] = one_hot_columns(low, 256)
    packed = dot(hot[...], wide[...]).astype(BF16)
    for k in range(8):
        out_ref[k] = packed[(k % 2) * LANES : (k % 2 + 1) * LANES, (k // 2) * LANES : (k // 2 + 1) * LANES]


def rel_sum(e, ids, rows):
    return kernel_call(
        rel_sum_body,
        shape((8, LANES, LANES), BF16),
        (SMEM,) + (VMEM,) * 8,
        scratch=[
            pltpu.VMEM((2048, FOLD * LANES), BF16),
            pltpu.VMEM((256, 2048), BF16),
        ],
        name="rel_sum",
        flops=1 << 29,
    )(e, *ids, *rows)


def rel_total_body(parts_ref, total_ref, square_ref):
    total = parts_ref[0].astype(F32)
    for k in range(1, Z):
        total += parts_ref[k].astype(F32)
    total_ref[...] = total
    square = jnp.sum(jnp.transpose(total * total), axis=0, keepdims=True)
    square_ref[...] = jnp.broadcast_to(square, (8, LANES))


def rel_total(parts):
    outs = (shape((LANES, LANES), F32), shape((8, LANES), F32))
    return kernel_call(rel_total_body, outs, (VMEM,), name="rel_total")(parts)


def rel_update_body(e_ref, total_ref, square_ref, state_ref, out_ref):
    state = state_ref[pl.ds(e_ref[0], 1), :]
    root = lax.sqrt(state + square_ref[:1, :] / (2 * RANK))
    out_ref[...] = (total_ref[...] * column(LEARN_RATE / root)).astype(BF16)


def rel_update(e, total, square, state):
    return kernel_call(
        rel_update_body, shape((LANES, LANES), BF16), (SMEM, VMEM, VMEM, VMEM), name="rel_update"
    )(e, total, square, state)


def rel_join_body(e_ref, *refs):
    z = e_ref[0] & 7
    for s in range(8):
        refs[8][(z + 8 - s) & 7] = refs[s][...]


def rel_join(e, parts):
    return kernel_call(
        rel_join_body, shape((8, LANES, LANES), BF16), (SMEM,) + (VMEM,) * 8, name="rel_join"
    )(e, *parts)


def rel_step_body(e_ref, table_ref, *refs):
    out_hbm, out_ref, sems = refs[4:]
    y = e_ref[0] >> 3
    copies = []
    for s in range(4):
        for half in range(2):
            first = ((y + 4 - s) & 3) * 1024 + half * 512
            at = pl.ds(pl.multiple_of(first, 512), 512)
            part = refs[s][half * 512 : (half + 1) * 512, :]
            out_ref[at, :] = table_ref[at, :] - part.astype(F32)
            copies.append(started(out_ref.at[at], out_hbm.at[at], sems.at[2 * s + half]))
    for copy in copies:
        copy.wait()


def rel_step(e, table, parts):
    return kernel_call(
        rel_step_body,
        shape(table.shape, F32),
        (SMEM,) + (VMEM,) * 5,
        scratch=[pltpu.VMEM(table.shape, F32), pltpu.SemaphoreType.DMA((8,))],
        out_specs=HBM,
        name="rel_step",
        flops=1 << 20,
    )(e, table, *parts)


Z_GROUPS = [[y * Z + z for z in range(Z)] for y in range(Y)]


def y_turn(s):
    return [(y * Z + z, (y + s) % Y * Z + z) for y in range(Y) for z in range(Z)]


def z_turn(s):
    return [(y * Z + z, y * Z + (z + s) % Z) for y in range(Y) for z in range(Z)]


X_MIRROR = [(x * 2 + c, (X - 1 - x) * 2 + c) for x in range(X) for c in range(2)]


def flip(bit):
    return [(i, i ^ bit) for i in range(X * CORES)]


def around(array, axis, turn, count):
    return [array] + [lax.ppermute(array, axis, turn(s)) for s in range(1, count)]


def summed_over_dim(values):
    for bit in (1, 2, 4):
        values = values + lax.ppermute(values, "dim", flip(bit))
    return values


def per_device(entities, ent_state, buckets, relations, rel_state, triples, negatives):
    rows_here = entities.shape[0]
    e = lax.axis_index("ent").reshape(1)
    core = (lax.axis_index("dim") & 1).reshape(1)
    slots, out_ids, rel_ids = place(core, triples, negatives)
    table = fold_table(entities)
    ids = lax.all_to_all(out_ids, "ent", 0, 0, tiled=True)
    arrived = lax.all_to_all(look_up(ids, table), "ent", 0, 0, tiled=True)
    near_ids = around(rel_ids, "ent", y_turn, Y)
    rel = jnp.take(relations, rel_ids.reshape(-1), axis=0, mode="clip")
    rel = rel.reshape(2, GROUP, LANES)
    flat = ids.reshape(-1) - 1
    counts = jnp.sum(
        (flat[:, None] == jnp.arange(rows_here, dtype=I32)[None, :]).astype(F32), axis=0
    )
    weight = REG_WEIGHT * (buckets.astype(F32) + 1.0) * counts
    reg = weight[:, None] * 3.0 * entities * jnp.abs(entities)
    slots, reg, near_ids, rel, hot = lax.optimization_barrier(
        (slots, reg, near_ids, rel, spread(ids))
    )

    *sent, partial = score(1, arrived, slots, rel)
    swapped = lax.ppermute(partial, "dim", flip(1))
    *kept, partial = score(0, arrived, slots, rel)
    partial = added(partial, swapped)
    partial = added(partial, lax.ppermute(partial, "dim", flip(2)))
    coef = coefficients(partial, lax.ppermute(partial, "dim", X_MIRROR))
    coef_other = lax.ppermute(coef, "dim", flip(1))
    packed, rel_rows = gradients(coef, coef_other, kept, sent, rel, slots)
    near_rows = around(rel_rows, "ent", y_turn, Y)
    parts = rel_sum(e, near_ids, near_rows)
    parts = lax.all_to_all(parts, "ent", 0, 0, tiled=True, axis_index_groups=Z_GROUPS)
    total, square = rel_total(parts)
    packed, total, square = lax.optimization_barrier((packed, total, square))
    returned = lax.all_to_all(packed, "ent", 0, 0, tiled=True)
    square = summed_over_dim(square)
    update = rel_update(e, total, square, rel_state.reshape(OWNERS, LANES))
    joined = rel_join(e, around(update, "ent", z_turn, Z)).reshape(1024, LANES)
    new_relations = rel_step(e, relations, around(joined, "ent", y_turn, Y))

    ent_total, ent_square = accumulate(ids, returned, reg, hot)
    ent_square = summed_over_dim(ent_square)
    new_entities = entity_step(
        entities, ent_total, ent_state.reshape(rows_here // LANES, LANES), ent_square
    )
    return (new_entities, new_relations)


def solution(mesh):
    placed = (
        P("ent", "dim"),
        P("ent"),
        P("ent"),
        P(None, "dim"),
        P(),
        P(None, "ent"),
        P("ent", None),
    )
    return jax.shard_map(
        per_device,
        mesh=mesh,
        in_specs=placed,
        out_specs=(P("ent", "dim"), P(None, "dim")),
        check_vma=False,
    )
```

```python
import functools

import jax
import jax.numpy as jnp
from jax import lax
from jax.experimental import pallas as pl
from jax.experimental.pallas import tpu as pltpu
from jax.sharding import PartitionSpec as P

RANK = 512
HALF = 64
LANES = 128
LEARN_RATE = 0.1
REG_WEIGHT = 0.01
Y, Z, X, CORES = 4, 8, 4, 2
OWNERS = Y * Z
GROUP = 256
NEG = 256
REQ = 768
CAP = 64
SPLIT = 512
FOLD = 4
PART = 272
F32, BF16, I32 = jnp.float32, jnp.bfloat16, jnp.int32


VMEM = pl.BlockSpec(memory_space=pltpu.VMEM)
SMEM = pl.BlockSpec(memory_space=pltpu.SMEM)
HBM = pl.BlockSpec(memory_space=pltpu.HBM)


def iota(shape, dim):
    return lax.broadcasted_iota(I32, shape, dim)


def column(row):
    return jnp.transpose(jnp.broadcast_to(row, (LANES, LANES)))


def swap(values):
    return pltpu.roll(values, HALF, 1)


def low_half(shape):
    return iota(shape, 1) < HALF


def product(former, latter, sign=1.0):
    low = low_half(former.shape)
    turned = swap(latter)
    real = jnp.where(low, latter, turned)
    imag = jnp.where(low, -sign * turned, sign * latter)
    return former * real + swap(former) * imag


def dot(a, b, dims=((1,), (0,))):
    return lax.dot_general(a, b, (dims, ((), ())), preferred_element_type=F32)


def kernel_call(body, outs, ins, scratch=(), flops=0, limit=12, out_specs=None):
    out_specs = out_specs or jax.tree.map(lambda _: VMEM, outs)
    outs = jax.tree.map(
        lambda o, spec: pltpu.HBM(o.shape, o.dtype) if spec is HBM else o, outs, out_specs
    )

    def call(*args):
        args = [
            pltpu.with_memory_space_constraint(a, pltpu.HBM) if spec is HBM else a
            for a, spec in zip(args, ins)
        ]
        return pl.pallas_call(
            body,
            out_shape=outs,
            in_specs=list(ins),
            out_specs=out_specs,
            scratch_shapes=list(scratch),
            compiler_params=pltpu.CompilerParams(vmem_limit_bytes=limit << 20),
            cost_estimate=pl.CostEstimate(
                flops=flops,
                transcendentals=0,
                bytes_accessed=sum(a.size * a.dtype.itemsize for a in args),
            ),
        )(*args)

    return call


def started(source, target, sem):
    copy = pltpu.make_async_copy(source, target, sem)
    copy.start()
    return copy


def shape(dims, kind):
    return jax.ShapeDtypeStruct(dims, kind)


def one_hot_rows(col, count):
    tiles = [col == iota((LANES, LANES), 1) + LANES * j for j in range(count // LANES)]
    return jnp.concatenate([t.astype(F32).astype(BF16) for t in tiles], axis=1)


def one_hot_columns(row, count):
    return (iota((count, LANES), 0) == row).astype(F32).astype(BF16)


def unfold(wide, high):
    out = jnp.where(high == 0, wide[:, :LANES], 0.0)
    for j in range(1, FOLD):
        out = jnp.where(high == j, wide[:, j * LANES : (j + 1) * LANES], out)
    return out


def fold(rows, high):
    return jnp.concatenate(
        [jnp.where(high == j, rows, 0.0).astype(BF16) for j in range(FOLD)], axis=1
    )


def place_body(
    core_ref, triples_hbm, negatives_hbm, slots_ref, ids_ref, rel_ref, triples_ref, negatives_ref, sems
):
    copies = [
        started(triples_hbm, triples_ref, sems.at[0]),
        started(negatives_hbm, negatives_ref, sems.at[1]),
    ]
    blocks = REQ // LANES
    earlier = (iota((REQ, REQ), 0) < iota((REQ, REQ), 1)).astype(F32).astype(BF16)
    high_sum = jnp.zeros((OWNERS, LANES), F32)
    low_sum = jnp.zeros((OWNERS, LANES), F32)
    for copy in copies:
        copy.wait()
    for k in range(2):
        flip_groups = core_ref[0] != k

        def pick(ref, row, block, step):
            first = ref[row[0] : row[0] + 1, block * LANES : (block + 1) * LANES]
            block += step
            second = ref[row[1] : row[1] + 1, block * LANES : (block + 1) * LANES]
            return jnp.where(flip_groups, second, first)

        for c in range(2):
            rel_ref[2 * k + c : 2 * k + c + 1, :] = pick(triples_ref, (1, 1), c, 2)
        rows = [pick(triples_ref, (kind, kind), c, 2) for kind in (0, 2) for c in range(2)]
        rows += [pick(negatives_ref, (0, 1), c, 0) for c in range(2)]
        owner_hits = [iota((OWNERS, LANES), 0) == (row >> 11) for row in rows]
        hits = jnp.concatenate([h.astype(F32).astype(BF16) for h in owner_hits], axis=1)
        before = dot(hits, earlier)
        for b in range(blocks):
            row = rows[b]
            mine = before[:, b * LANES : (b + 1) * LANES]
            rank = jnp.sum(jnp.where(owner_hits[b], mine, 0.0), axis=0, keepdims=True)
            rank = rank.astype(I32)
            slots_ref[k, b : b + 1, :] = (row >> 11) * CAP + rank
            value = (row & 2047) + 1
            at = column(rank) + CAP * k == iota((LANES, LANES), 1)
            val = column(value)
            hit = hits[:, b * LANES : (b + 1) * LANES]
            high_sum += dot(hit, jnp.where(at, (val >> 6).astype(F32), 0.0).astype(BF16))
            low_sum += dot(hit, jnp.where(at, (val & 63).astype(F32), 0.0).astype(BF16))
    ids_ref[...] = (high_sum * 64.0 + low_sum).astype(I32)


def place(core, triples, negatives):
    outs = (
        shape((2, REQ // LANES, LANES), I32),
        shape((OWNERS, LANES), I32),
        shape((4, LANES), I32),
    )
    return kernel_call(
        place_body,
        outs,
        (SMEM, HBM, HBM),
        scratch=[
            pltpu.VMEM(triples.shape, I32),
            pltpu.VMEM(negatives.shape, I32),
            pltpu.SemaphoreType.DMA((2,)),
        ],
        flops=1 << 27,
    )(core, triples, negatives)


def fold_body(table_hbm, out_hbm, table_ref, out_ref, sems):
    copies = [
        started(
            table_hbm.at[j * SPLIT : (j + 1) * SPLIT],
            table_ref.at[j * SPLIT : (j + 1) * SPLIT],
            sems.at[j],
        )
        for j in range(FOLD)
    ]
    for j in range(FOLD):
        copies[j].wait()
        out_ref[:, j * LANES : (j + 1) * LANES] = table_ref[
            j * SPLIT : (j + 1) * SPLIT, :
        ].astype(BF16)
    started(out_ref, out_hbm, sems.at[FOLD]).wait()


def fold_table(table):
    return kernel_call(
        fold_body,
        shape((SPLIT, FOLD * LANES), BF16),
        (HBM,),
        scratch=[
            pltpu.VMEM(table.shape, F32),
            pltpu.VMEM((SPLIT, FOLD * LANES), BF16),
            pltpu.SemaphoreType.DMA((FOLD + 1,)),
        ],
        out_specs=HBM,
        flops=1 << 22,
    )(table)


def look_up_body(ids_ref, table_hbm, out_hbm, table_ref, rows, sems):
    started(table_hbm, table_ref, sems.at[OWNERS // 8]).wait()

    def leave(k):
        at = pl.ds(k * 8, 8)
        return pltpu.make_async_copy(rows.at[at], out_hbm.at[at], sems.at[k])

    def step(k, _):
        ids = ids_ref[pl.ds(pl.multiple_of(k * 8, 8), 8), :]
        for i in range(8):
            at = column(ids[i : i + 1, :]) - 1
            low = jnp.where(at >= 0, at & (SPLIT - 1), -1)
            wide = dot(one_hot_rows(low, SPLIT), table_ref[...])
            rows[k * 8 + i] = unfold(wide, at >> 9).astype(BF16)
        leave(k).start()
        return 0

    lax.fori_loop(0, OWNERS // 8, step, 0)
    for k in range(OWNERS // 8):
        leave(k).wait()


def look_up(ids, table):
    return kernel_call(
        look_up_body,
        shape((OWNERS, LANES, LANES), BF16),
        (VMEM, HBM),
        scratch=[
            pltpu.VMEM((SPLIT, FOLD * LANES), BF16),
            pltpu.VMEM((OWNERS, LANES, LANES), BF16),
            pltpu.SemaphoreType.DMA((OWNERS // 8 + 1,)),
        ],
        out_specs=HBM,
        flops=1 << 31,
    )(ids, table)


def spread_body(ids_ref, out_hbm, out_ref, sem):
    for i in range(OWNERS):
        row = ids_ref[i : i + 1, :] - 1
        low = jnp.where(row >= 0, row & (SPLIT - 1), -1)
        out_ref[:, i * LANES : (i + 1) * LANES] = one_hot_columns(low, SPLIT)
    started(out_ref, out_hbm, sem).wait()


def spread(ids):
    pairs = OWNERS * LANES
    return kernel_call(
        spread_body,
        shape((SPLIT, pairs), BF16),
        (VMEM,),
        scratch=[pltpu.VMEM((SPLIT, pairs), BF16), pltpu.SemaphoreType.DMA],
        out_specs=HBM,
        flops=1 << 22,
    )(ids)


def score_body(
    g, arrived_hbm, slots_ref, rel_ref, rows_ref, query_ref, probe_ref, out_ref, wide, sems
):
    copies = [
        started(
            arrived_hbm.at[j * 8 : (j + 1) * 8, g * CAP : (g + 1) * CAP, :],
            wide.at[:, :, j * LANES : (j + 1) * LANES],
            sems.at[j],
        )
        for j in range(FOLD)
    ]
    for copy in copies:
        copy.wait()
    table = wide[...].reshape(SPLIT, FOLD * LANES)
    for b in range(REQ // LANES):
        at = column(slots_ref[g, b : b + 1, :])
        picked = dot(one_hot_rows(at & (SPLIT - 1), SPLIT), table)
        rows_ref[b * LANES : (b + 1) * LANES, :] = unfold(picked, at >> 9).astype(BF16)
    head = rows_ref[:GROUP, :].astype(F32)
    tail = rows_ref[GROUP : 2 * GROUP, :].astype(F32)
    noise = rows_ref[2 * GROUP :, :]
    rel = rel_ref[g].astype(BF16).astype(F32)
    query = product(head, rel).astype(BF16)
    probe = product(tail, rel, -1.0).astype(BF16)
    query_ref[...] = query
    probe_ref[...] = probe
    pos = jnp.sum(jnp.transpose(query.astype(F32) * tail), axis=0, keepdims=True)
    for side, left in enumerate((query, probe)):
        both = dot(left, noise, ((1,), (1,))).astype(BF16)
        for q in range(4):
            for c in range(2):
                out_ref[q, (2 * side + c) * 64 : (2 * side + c + 1) * 64, :] = both[
                    q * 64 : (q + 1) * 64, c * LANES : (c + 1) * LANES
                ]
    for q in range(4):
        row = pos[:, (q // 2) * LANES : (q // 2 + 1) * LANES]
        out_ref[q, 256:PART, :] = jnp.broadcast_to(row, (PART - 256, LANES)).astype(BF16)


def score(g, arrived, slots, rel):
    outs = (
        shape((REQ, LANES), BF16),
        shape((GROUP, LANES), BF16),
        shape((GROUP, LANES), BF16),
        shape((4, PART, LANES), BF16),
    )
    return kernel_call(
        functools.partial(score_body, g),
        outs,
        (HBM, VMEM, VMEM),
        scratch=[
            pltpu.VMEM((8, CAP, FOLD * LANES), BF16),
            pltpu.SemaphoreType.DMA((FOLD,)),
        ],
        flops=1 << 29,
    )(arrived, slots, rel)


def split_body(kept_ref, other_ref, near_ref, far_ref):
    for half, ref in enumerate((near_ref, far_ref)):
        at = slice(2 * half, 2 * half + 2)
        ref[...] = (kept_ref[at].astype(F32) + other_ref[at].astype(F32)).astype(BF16)


def split_sum(kept, other):
    half = shape((2, PART, LANES), BF16)
    return kernel_call(split_body, (half, half), (VMEM, VMEM))(kept, other)


def add_body(a_ref, b_ref, c_ref, d_ref, near_ref, far_ref):
    near_ref[...] = (a_ref[...].astype(F32) + b_ref[...].astype(F32)).astype(BF16)
    far_ref[...] = (c_ref[...].astype(F32) + d_ref[...].astype(F32)).astype(BF16)


def added(*parts):
    half = shape((2, PART, LANES), BF16)
    return kernel_call(add_body, (half, half), (VMEM,) * 4)(*parts)


def coef_body(a_ref, b_ref, c_ref, d_ref, out_ref):
    for half, (left, right) in enumerate(((a_ref, b_ref), (c_ref, d_ref))):
        for q in range(2):
            total = left[q].astype(F32) + right[q].astype(F32)
            at = 2 * half + q
            out_ref[at, :256, :] = (jax.nn.sigmoid(total[:256, :]) / NEG).astype(BF16)
            out_ref[at, 256:, :] = (-jax.nn.sigmoid(-total[256:, :])).astype(BF16)


def coefficients(*parts):
    return kernel_call(coef_body, shape((4, PART, LANES), BF16), (VMEM,) * 4)(*parts)


def grad_body(mine_ref, other_ref, rows0, query0, probe0, rows1, query1, probe1, *refs):
    rel_ref, ids_ref, grads_ref, relrow_ref, tail_c, head_c = refs
    ids = ids_ref[...]
    coded = jnp.concatenate([ids >> 6, ids & 63, ids, ids], axis=0)
    relrow_ref[2 * GROUP :, :] = coded.astype(F32).astype(BF16)
    groups = ((mine_ref, rows0, query0, probe0), (other_ref, rows1, query1, probe1))
    for g, (coef_ref, rows_ref, query_ref, probe_ref) in enumerate(groups):
        for q in range(4):
            at = slice(q * 64, (q + 1) * 64)
            for c in range(2):
                lanes = slice(c * LANES, (c + 1) * LANES)
                tail_c[at, lanes] = coef_ref[q, c * 64 : (c + 1) * 64, :]
                head_c[at, lanes] = coef_ref[q, (2 + c) * 64 : (3 + c) * 64, :]
        pos = [column(coef_ref[q, 256:PART, :].astype(F32)[:1, :]) for q in (0, 2)]
        pos = jnp.concatenate(pos, axis=0)
        head = rows_ref[:GROUP, :].astype(F32)
        tail = rows_ref[GROUP : 2 * GROUP, :].astype(F32)
        noise = rows_ref[2 * GROUP :, :]
        rel = rel_ref[g].astype(BF16).astype(F32)
        tail_pull = pos * tail + dot(tail_c[...], noise)
        head_pull = dot(head_c[...], noise)
        head_side = pos * head + head_pull
        head_grad = product(tail_pull, rel, -1.0)
        tail_grad = product(head_side, rel)
        noise_grad = dot(tail_c[...], query_ref[...], ((0,), (0,))) + dot(
            head_c[...], probe_ref[...], ((0,), (0,))
        )
        relrow_ref[g * GROUP : (g + 1) * GROUP, :] = (
            product(tail_pull, head, -1.0) + product(tail, head_pull, -1.0)
        ).astype(BF16)
        grads_ref[g, :GROUP, :] = head_grad.astype(BF16)
        grads_ref[g, GROUP : 2 * GROUP, :] = tail_grad.astype(BF16)
        grads_ref[g, 2 * GROUP :, :] = noise_grad.astype(BF16)


def gradients(mine, other, kept, sent, rel, rel_ids):
    outs = (shape((2, REQ, LANES), BF16), shape((2 * GROUP + 16, LANES), BF16))
    return kernel_call(
        grad_body,
        outs,
        (VMEM,) * 10,
        scratch=[pltpu.VMEM((GROUP, NEG), BF16), pltpu.VMEM((GROUP, NEG), BF16)],
        flops=1 << 29,
    )(mine, other, *kept, *sent, rel, rel_ids)


def pack_body(grads_ref, slots_ref, out_hbm, out_ref, wide, hot, sems):
    copies = []
    for g in range(2):
        for b in range(REQ // LANES):
            row = slots_ref[g, b : b + 1, :]
            at = slice(b * LANES, (b + 1) * LANES)
            wide[at, :] = fold(grads_ref[g, at, :].astype(F32), column(row) >> 9)
            hot[:, at] = one_hot_columns(row & (SPLIT - 1), SPLIT)
        for k in range(SPLIT // LANES):
            packed = dot(hot[k * LANES : (k + 1) * LANES, :], wide[...])
            for j in range(FOLD):
                piece = packed[:, j * LANES : (j + 1) * LANES].astype(BF16)
                first = j * 8 + k * 2
                out_ref[g, first : first + 2] = piece.reshape(2, CAP, LANES)
        copies.append(started(out_ref.at[g], out_hbm.at[:, g * CAP : (g + 1) * CAP, :], sems.at[g]))
    for copy in copies:
        copy.wait()


def pack(grads, slots):
    return kernel_call(
        pack_body,
        shape((OWNERS, 2 * CAP, LANES), BF16),
        (VMEM, VMEM),
        scratch=[
            pltpu.VMEM((2, OWNERS, CAP, LANES), BF16),
            pltpu.VMEM((REQ, FOLD * LANES), BF16),
            pltpu.VMEM((SPLIT, REQ), BF16),
            pltpu.SemaphoreType.DMA((2,)),
        ],
        out_specs=HBM,
        flops=1 << 30,
    )(grads, slots)


def accumulate_body(
    ids_ref, back_hbm, reg_hbm, hot_hbm, total_hbm, square_ref,
    back_ref, reg_ref, hot, wide, total_ref, sems,
):
    pieces = 4
    step = OWNERS // pieces
    width = step * LANES
    backs, hots = [], []
    for k in range(pieces):
        at = slice(k * step, (k + 1) * step)
        backs.append(started(back_hbm.at[at], back_ref.at[at], sems.at[k]))
        at = slice(k * width, (k + 1) * width)
        hots.append(started(hot_hbm.at[:, at], hot.at[:, at], sems.at[pieces + k]))
    reg_copy = started(reg_hbm, reg_ref, sems.at[2 * pieces])
    for k in range(pieces):
        backs[k].wait()

        def spread_rows(i, _, k=k):
            at = k * step + i
            row = ids_ref[pl.ds(at, 1), :] - 1
            wide[pl.ds(pl.multiple_of(at * LANES, LANES), LANES), :] = fold(
                back_ref[at].astype(F32), column(row) >> 9
            )
            return 0

        lax.fori_loop(0, step, spread_rows, 0, unroll=4)
    for k in range(pieces):
        hots[k].wait()
    reg_copy.wait()
    copies = []
    for m in range(SPLIT // LANES):
        packed = dot(hot[m * LANES : (m + 1) * LANES, :], wide[...])
        for j in range(FOLD):
            at = slice(j * SPLIT + m * LANES, j * SPLIT + (m + 1) * LANES)
            total = packed[:, j * LANES : (j + 1) * LANES] + reg_ref[at, :]
            total_ref[at, :] = total
            row = j * FOLD + m
            square_ref[row : row + 1, :] = jnp.sum(
                jnp.transpose(total * total), axis=0, keepdims=True
            )
            copies.append(started(total_ref.at[at], total_hbm.at[at], sems.at[9 + 4 * m + j]))
    for copy in copies:
        copy.wait()


def accumulate(ids, back, reg, hot):
    rows = FOLD * SPLIT
    pairs = OWNERS * LANES
    return kernel_call(
        accumulate_body,
        (shape((rows, LANES), F32), shape((rows // LANES, LANES), F32)),
        (VMEM, HBM, HBM, HBM),
        scratch=[
            pltpu.VMEM((OWNERS, LANES, LANES), BF16),
            pltpu.VMEM((rows, LANES), F32),
            pltpu.VMEM((SPLIT, pairs), BF16),
            pltpu.VMEM((pairs, FOLD * LANES), BF16),
            pltpu.VMEM((rows, LANES), F32),
            pltpu.SemaphoreType.DMA((25,)),
        ],
        out_specs=(HBM, VMEM),
        flops=1 << 31,
        limit=24,
    )(ids, back, reg, hot)


def step_body(table_hbm, total_hbm, state_ref, square_ref, out_hbm, table_ref, total_ref, sems):
    pieces = 4
    rows = table_ref.shape[0] // pieces
    tables, totals, outs = [], [], []
    for k in range(pieces):
        at = slice(k * rows, (k + 1) * rows)
        tables.append(started(table_hbm.at[at], table_ref.at[at], sems.at[3 * k]))
        totals.append(started(total_hbm.at[at], total_ref.at[at], sems.at[3 * k + 1]))
    count = table_ref.shape[0] // LANES
    scale = LEARN_RATE / lax.sqrt(state_ref[...] + square_ref[:count, :] / (2 * RANK))
    for k in range(pieces):
        tables[k].wait()
        totals[k].wait()
        for b in range(k * rows // LANES, (k + 1) * rows // LANES):
            at = slice(b * LANES, (b + 1) * LANES)
            table_ref[at, :] = table_ref[at, :] - total_ref[at, :] * column(scale[b : b + 1, :])
        at = slice(k * rows, (k + 1) * rows)
        outs.append(started(table_ref.at[at], out_hbm.at[at], sems.at[3 * k + 2]))
    for copy in outs:
        copy.wait()


def entity_step(table, total, state, square):
    return kernel_call(
        step_body,
        shape(table.shape, F32),
        (HBM, HBM, VMEM, VMEM),
        scratch=[
            pltpu.VMEM(table.shape, F32),
            pltpu.VMEM(table.shape, F32),
            pltpu.SemaphoreType.DMA((12,)),
        ],
        out_specs=HBM,
    )(table, total, state, square)


def rel_sum_body(e_ref, *refs):
    rows, outs, wide, hot, total = refs[:4], refs[4:12], refs[12], refs[13], refs[14]
    y = e_ref[0] >> 3
    z = e_ref[0] & 7
    for s in range(4):
        coded = rows[s][2 * GROUP :, :].astype(F32)
        ids = (coded[:4] * 64.0 + coded[4:8]).astype(I32) - y * 1024
        for b in range(4):
            row = ids[b : b + 1, :]
            inside = (row >= 0) & (row < 1024)
            low = jnp.where(inside, row & 255, -1)
            at = slice(s * 512 + b * LANES, s * 512 + (b + 1) * LANES)
            wide[at, :] = fold(rows[s][b * LANES : (b + 1) * LANES, :].astype(F32), column(row) >> 8)
            hot[:, at] = one_hot_columns(low, 256)
    packed = dot(hot[...], wide[...]).astype(BF16)
    for k in range(8):
        total[k] = packed[
            (k % 2) * LANES : (k % 2 + 1) * LANES, (k // 2) * LANES : (k // 2 + 1) * LANES
        ]
    for s in range(8):
        outs[s][...] = total[(z + s) & 7]


def rel_sum(e, rows):
    return kernel_call(
        rel_sum_body,
        tuple(shape((LANES, LANES), BF16) for _ in range(8)),
        (SMEM,) + (VMEM,) * 4,
        scratch=[
            pltpu.VMEM((2048, FOLD * LANES), BF16),
            pltpu.VMEM((256, 2048), BF16),
            pltpu.VMEM((8, LANES, LANES), BF16),
        ],
        flops=1 << 29,
    )(e, *rows)


def rel_total_body(*refs):
    out_hbm, total_ref, sems = refs[8:]
    total = refs[0][...].astype(F32)
    for ref in refs[1:8]:
        total += ref[...].astype(F32)
    total_ref[...] = total.astype(BF16)
    for copy in [started(total_ref, out_hbm.at[k], sems.at[k]) for k in range(8)]:
        copy.wait()


def rel_total(parts):
    return kernel_call(
        rel_total_body,
        shape((8, LANES, LANES), BF16),
        (VMEM,) * 8,
        scratch=[pltpu.VMEM((LANES, LANES), BF16), pltpu.SemaphoreType.DMA((8,))],
        out_specs=HBM,
    )(*parts)


def squares_body(total_ref, out_ref):
    for k in range(8):
        total = total_ref[k].astype(F32)
        out_ref[k : k + 1, :] = jnp.sum(jnp.transpose(total * total), axis=0, keepdims=True)


def squares_of(total):
    return kernel_call(squares_body, shape((8, LANES), F32), (VMEM,))(total)


def rel_step_body(e_ref, table_ref, state_ref, *refs):
    square_refs, (out_hbm, out_ref, sems) = refs[4:8], refs[8:]
    y = e_ref[0] >> 3
    copies = []
    for s in range(4):
        quarter = (y + 4 - s) & 3
        state = state_ref[pl.ds(pl.multiple_of(quarter * 8, 8), 8), :]
        square = square_refs[s][...]
        scale = LEARN_RATE / lax.sqrt(state + square / (2 * RANK))
        for k in range(8):
            at = pl.ds(pl.multiple_of(quarter * 1024 + k * LANES, LANES), LANES)
            grad = refs[s][k].astype(F32)
            out_ref[at, :] = table_ref[at, :] - grad * column(scale[k : k + 1, :])
        at = pl.ds(pl.multiple_of(quarter * 1024, 1024), 1024)
        copies.append(started(out_ref.at[at], out_hbm.at[at], sems.at[s]))
    for copy in copies:
        copy.wait()


def rel_step(e, table, state, parts, squares):
    return kernel_call(
        rel_step_body,
        shape(table.shape, F32),
        (SMEM,) + (VMEM,) * 10,
        scratch=[pltpu.VMEM(table.shape, F32), pltpu.SemaphoreType.DMA((4,))],
        out_specs=HBM,
        flops=1 << 20,
    )(e, table, state, *parts, *squares)


Z_GROUPS = [[y * Z + z for z in range(Z)] for y in range(Y)]


def y_turn(s):
    return [(y * Z + z, (y + s) % Y * Z + z) for y in range(Y) for z in range(Z)]


def z_turn(s):
    return [(y * Z + z, y * Z + (z + s) % Z) for y in range(Y) for z in range(Z)]


X_MIRROR = [(x * 2 + c, (X - 1 - x) * 2 + c) for x in range(X) for c in range(2)]


def flip(bit):
    return [(i, i ^ bit) for i in range(X * CORES)]


def around(array, axis, turn, count):
    return [array] + [lax.ppermute(array, axis, turn(s)) for s in range(1, count)]


def scattered(parts, axis, turn):
    return [parts[0]] + [lax.ppermute(p, axis, turn(s)) for s, p in enumerate(parts) if s]


def summed_over_dim(values):
    for turn in (flip(1), flip(2), X_MIRROR):
        values = values + lax.ppermute(values, "dim", turn)
    return values


def per_device(entities, ent_state, buckets, relations, rel_state, triples, negatives):
    rows_here = entities.shape[0]
    e = lax.axis_index("ent").reshape(1)
    core = (lax.axis_index("dim") & 1).reshape(1)
    slots, out_ids, rel_ids = place(core, triples, negatives)
    table = fold_table(entities)
    ids = lax.all_to_all(out_ids, "ent", 0, 0, tiled=True)
    arrived = lax.all_to_all(look_up(ids, table), "ent", 0, 0, tiled=True)
    rel = jnp.take(relations, rel_ids.reshape(-1), axis=0, mode="clip")
    rel = rel.reshape(2, GROUP, LANES)
    flat = ids.reshape(-1) - 1
    counts = jnp.sum(
        (flat[:, None] == jnp.arange(rows_here, dtype=I32)[None, :]).astype(F32), axis=0
    )
    weight = REG_WEIGHT * (buckets.astype(F32) + 1.0) * counts
    reg = weight[:, None] * 3.0 * entities * jnp.abs(entities)
    slots, reg, rel, hot = lax.optimization_barrier((slots, reg, rel, spread(ids)))

    *sent, partial = score(1, arrived, slots, rel)
    swapped = lax.ppermute(partial, "dim", flip(1))
    *kept, partial = score(0, arrived, slots, rel)
    near, far = split_sum(partial, swapped)
    near, far = added(
        near, lax.ppermute(near, "dim", flip(2)), far, lax.ppermute(far, "dim", X_MIRROR)
    )
    coef = coefficients(
        near, lax.ppermute(near, "dim", X_MIRROR), far, lax.ppermute(far, "dim", flip(2))
    )
    coef_other = lax.ppermute(coef, "dim", flip(1))
    grads, rel_rows = gradients(coef, coef_other, kept, sent, rel, rel_ids)
    packed = pack(grads, slots)
    near_rows = around(rel_rows, "ent", y_turn, Y)
    returned = lax.all_to_all(packed, "ent", 0, 0, tiled=True)
    parts = rel_sum(e, near_rows)
    parts = scattered(parts, "ent", z_turn)
    total = rel_total(parts)
    joined = lax.all_to_all(total, "ent", 0, 0, tiled=True, axis_index_groups=Z_GROUPS)
    near_totals = around(joined, "ent", y_turn, Y)
    ent_total, ent_square = accumulate(ids, returned, reg, hot)
    squares = jnp.concatenate([ent_square, squares_of(joined)], axis=0)
    squares = summed_over_dim(squares)
    rel_squares = around(squares[rows_here // LANES :], "ent", y_turn, Y)
    new_relations = rel_step(
        e, relations, rel_state.reshape(OWNERS, LANES), near_totals, rel_squares
    )
    new_entities = entity_step(
        entities, ent_total, ent_state.reshape(rows_here // LANES, LANES), squares
    )
    return (new_entities, new_relations)


def solution(mesh):
    placed = (
        P("ent", "dim"),
        P("ent"),
        P("ent"),
        P(None, "dim"),
        P(),
        P(None, "ent"),
        P("ent", None),
    )
    return jax.shard_map(
        per_device,
        mesh=mesh,
        in_specs=placed,
        out_specs=(P("ent", "dim"), P(None, "dim")),
        check_vma=False,
    )
```

```python
import functools

import jax
import jax.numpy as jnp
from jax import lax
from jax.experimental import pallas as pl
from jax.experimental.pallas import tpu as pltpu
from jax.sharding import PartitionSpec as P

RANK = 512
HALF = 64
LANES = 128
LEARN_RATE = 0.1
REG_WEIGHT = 0.01
Y, Z, X, CORES = 4, 8, 4, 2
OWNERS = Y * Z
GROUP = 256
NEG = 256
REQ = 768
CAP = 64
SPLIT = 512
FOLD = 4
PART = 272
F32, BF16, I32 = jnp.float32, jnp.bfloat16, jnp.int32


VMEM = pl.BlockSpec(memory_space=pltpu.VMEM)
SMEM = pl.BlockSpec(memory_space=pltpu.SMEM)
HBM = pl.BlockSpec(memory_space=pltpu.HBM)


def iota(shape, dim):
    return lax.broadcasted_iota(I32, shape, dim)


def column(row):
    return jnp.transpose(jnp.broadcast_to(row, (LANES, LANES)))


def swap(values):
    return pltpu.roll(values, HALF, 1)


def low_half(shape):
    return iota(shape, 1) < HALF


def product(former, latter, sign=1.0):
    low = low_half(former.shape)
    turned = swap(latter)
    real = jnp.where(low, latter, turned)
    imag = jnp.where(low, -sign * turned, sign * latter)
    return former * real + swap(former) * imag


def dot(a, b, dims=((1,), (0,))):
    return lax.dot_general(a, b, (dims, ((), ())), preferred_element_type=F32)


def kernel_call(body, outs, ins, scratch=(), flops=0, limit=12, out_specs=None):
    out_specs = out_specs or jax.tree.map(lambda _: VMEM, outs)
    outs = jax.tree.map(
        lambda o, spec: pltpu.HBM(o.shape, o.dtype) if spec is HBM else o, outs, out_specs
    )

    def call(*args):
        args = [
            pltpu.with_memory_space_constraint(a, pltpu.HBM) if spec is HBM else a
            for a, spec in zip(args, ins)
        ]
        return pl.pallas_call(
            body,
            out_shape=outs,
            in_specs=list(ins),
            out_specs=out_specs,
            scratch_shapes=list(scratch),
            compiler_params=pltpu.CompilerParams(vmem_limit_bytes=limit << 20),
            cost_estimate=pl.CostEstimate(
                flops=flops,
                transcendentals=0,
                bytes_accessed=sum(a.size * a.dtype.itemsize for a in args),
            ),
        )(*args)

    return call


def started(source, target, sem):
    copy = pltpu.make_async_copy(source, target, sem)
    copy.start()
    return copy


def shape(dims, kind):
    return jax.ShapeDtypeStruct(dims, kind)


def one_hot_rows(col, count):
    tiles = [col == iota((LANES, LANES), 1) + LANES * j for j in range(count // LANES)]
    return jnp.concatenate([t.astype(F32).astype(BF16) for t in tiles], axis=1)


def one_hot_columns(row, count):
    return (iota((count, LANES), 0) == row).astype(F32).astype(BF16)


def unfold(wide, high):
    out = jnp.where(high == 0, wide[:, :LANES], 0.0)
    for j in range(1, FOLD):
        out = jnp.where(high == j, wide[:, j * LANES : (j + 1) * LANES], out)
    return out


def fold(rows, high):
    return jnp.concatenate(
        [jnp.where(high == j, rows, 0.0).astype(BF16) for j in range(FOLD)], axis=1
    )


def place_body(
    core_ref, triples_hbm, negatives_hbm, slots_ref, ids_ref, rel_ref, triples_ref, negatives_ref, sems
):
    copies = [
        started(triples_hbm, triples_ref, sems.at[0]),
        started(negatives_hbm, negatives_ref, sems.at[1]),
    ]
    blocks = REQ // LANES
    earlier = (iota((REQ, REQ), 0) < iota((REQ, REQ), 1)).astype(F32).astype(BF16)
    high_sum = jnp.zeros((OWNERS, LANES), F32)
    low_sum = jnp.zeros((OWNERS, LANES), F32)
    for copy in copies:
        copy.wait()
    for k in range(2):
        flip_groups = core_ref[0] != k

        def pick(ref, row, block, step):
            first = ref[row[0] : row[0] + 1, block * LANES : (block + 1) * LANES]
            block += step
            second = ref[row[1] : row[1] + 1, block * LANES : (block + 1) * LANES]
            return jnp.where(flip_groups, second, first)

        for c in range(2):
            rel_ref[2 * k + c : 2 * k + c + 1, :] = pick(triples_ref, (1, 1), c, 2)
        rows = [pick(triples_ref, (kind, kind), c, 2) for kind in (0, 2) for c in range(2)]
        rows += [pick(negatives_ref, (0, 1), c, 0) for c in range(2)]
        owner_hits = [iota((OWNERS, LANES), 0) == (row >> 11) for row in rows]
        hits = jnp.concatenate([h.astype(F32).astype(BF16) for h in owner_hits], axis=1)
        before = dot(hits, earlier)
        for b in range(blocks):
            row = rows[b]
            mine = before[:, b * LANES : (b + 1) * LANES]
            rank = jnp.sum(jnp.where(owner_hits[b], mine, 0.0), axis=0, keepdims=True)
            rank = rank.astype(I32)
            slots_ref[k, b : b + 1, :] = (row >> 11) * CAP + rank
            value = (row & 2047) + 1
            at = column(rank) + CAP * k == iota((LANES, LANES), 1)
            val = column(value)
            hit = hits[:, b * LANES : (b + 1) * LANES]
            high_sum += dot(hit, jnp.where(at, (val >> 6).astype(F32), 0.0).astype(BF16))
            low_sum += dot(hit, jnp.where(at, (val & 63).astype(F32), 0.0).astype(BF16))
    ids_ref[...] = (high_sum * 64.0 + low_sum).astype(I32)


def place(core, triples, negatives):
    outs = (
        shape((2, REQ // LANES, LANES), I32),
        shape((OWNERS, LANES), I32),
        shape((4, LANES), I32),
    )
    return kernel_call(
        place_body,
        outs,
        (SMEM, HBM, HBM),
        scratch=[
            pltpu.VMEM(triples.shape, I32),
            pltpu.VMEM(negatives.shape, I32),
            pltpu.SemaphoreType.DMA((2,)),
        ],
        flops=1 << 27,
    )(core, triples, negatives)


def fold_body(table_hbm, out_hbm, table_ref, out_ref, sems):
    copies = [
        started(
            table_hbm.at[j * SPLIT : (j + 1) * SPLIT],
            table_ref.at[j * SPLIT : (j + 1) * SPLIT],
            sems.at[j],
        )
        for j in range(FOLD)
    ]
    for j in range(FOLD):
        copies[j].wait()
        out_ref[:, j * LANES : (j + 1) * LANES] = table_ref[
            j * SPLIT : (j + 1) * SPLIT, :
        ].astype(BF16)
    started(out_ref, out_hbm, sems.at[FOLD]).wait()


def fold_table(table):
    return kernel_call(
        fold_body,
        shape((SPLIT, FOLD * LANES), BF16),
        (HBM,),
        scratch=[
            pltpu.VMEM(table.shape, F32),
            pltpu.VMEM((SPLIT, FOLD * LANES), BF16),
            pltpu.SemaphoreType.DMA((FOLD + 1,)),
        ],
        out_specs=HBM,
        flops=1 << 22,
    )(table)


def look_up_body(ids_ref, table_hbm, out_hbm, table_ref, rows, hot, sems):
    chunk = 8
    table_copy = started(table_hbm, table_ref, sems.at[OWNERS // chunk])
    copies = []
    for first in range(0, OWNERS, chunk):
        high = []
        for i in range(chunk):
            at = column(ids_ref[first + i : first + i + 1, :]) - 1
            low = jnp.where(at >= 0, at & (SPLIT - 1), -1)
            hot[i * LANES : (i + 1) * LANES, :] = one_hot_rows(low, SPLIT)
            high.append(at >> 9)
        if first == 0:
            table_copy.wait()
        wide = dot(hot[...], table_ref[...])
        for i in range(chunk):
            picked = wide[i * LANES : (i + 1) * LANES, :]
            rows[first + i] = unfold(picked, high[i]).astype(BF16)
        at = slice(first, first + chunk)
        copies.append(started(rows.at[at], out_hbm.at[at], sems.at[first // chunk]))
    for copy in copies:
        copy.wait()


def look_up(ids, table):
    return kernel_call(
        look_up_body,
        shape((OWNERS, LANES, LANES), BF16),
        (VMEM, HBM),
        scratch=[
            pltpu.VMEM((SPLIT, FOLD * LANES), BF16),
            pltpu.VMEM((OWNERS, LANES, LANES), BF16),
            pltpu.VMEM((8 * LANES, SPLIT), BF16),
            pltpu.SemaphoreType.DMA((OWNERS // 8 + 1,)),
        ],
        out_specs=HBM,
        flops=1 << 31,
    )(ids, table)


def spread_body(ids_ref, out_hbm, out_ref, sem):
    def step(i, _):
        row = ids_ref[pl.ds(i, 1), :] - 1
        low = jnp.where(row >= 0, row & (SPLIT - 1), -1)
        at = pl.ds(pl.multiple_of(i * LANES, LANES), LANES)
        out_ref[:, at] = one_hot_columns(low, SPLIT)
        return 0

    lax.fori_loop(0, OWNERS, step, 0, unroll=2)
    started(out_ref, out_hbm, sem).wait()


def spread(ids):
    pairs = OWNERS * LANES
    return kernel_call(
        spread_body,
        shape((SPLIT, pairs), BF16),
        (VMEM,),
        scratch=[pltpu.VMEM((SPLIT, pairs), BF16), pltpu.SemaphoreType.DMA],
        out_specs=HBM,
        flops=1 << 22,
    )(ids)


def score_body(
    g, arrived_ref, slots_ref, rel_ref, rows_ref, query_ref, probe_ref, out_ref, wide
):
    for j in range(FOLD):
        part = arrived_ref[j * 8 : (j + 1) * 8, g * CAP : (g + 1) * CAP, :]
        wide[:, j * LANES : (j + 1) * LANES] = part.reshape(SPLIT, LANES)
    table = wide[...]
    for b in range(REQ // LANES):
        at = column(slots_ref[g, b : b + 1, :])
        picked = dot(one_hot_rows(at & (SPLIT - 1), SPLIT), table)
        rows_ref[b * LANES : (b + 1) * LANES, :] = unfold(picked, at >> 9).astype(BF16)
    head = rows_ref[:GROUP, :].astype(F32)
    tail = rows_ref[GROUP : 2 * GROUP, :].astype(F32)
    noise = rows_ref[2 * GROUP :, :]
    rel = rel_ref[g].astype(BF16).astype(F32)
    query = product(head, rel).astype(BF16)
    probe = product(tail, rel, -1.0).astype(BF16)
    query_ref[...] = query
    probe_ref[...] = probe
    pos = jnp.sum(jnp.transpose(query.astype(F32) * tail), axis=0, keepdims=True)
    for side, left in enumerate((query, probe)):
        both = dot(left, noise, ((1,), (1,))).astype(BF16)
        for q in range(4):
            for c in range(2):
                out_ref[q, (2 * side + c) * 64 : (2 * side + c + 1) * 64, :] = both[
                    q * 64 : (q + 1) * 64, c * LANES : (c + 1) * LANES
                ]
    for q in range(4):
        row = pos[:, (q // 2) * LANES : (q // 2 + 1) * LANES]
        out_ref[q, 256:PART, :] = jnp.broadcast_to(row, (PART - 256, LANES)).astype(BF16)


def score(g, arrived, slots, rel):
    outs = (
        shape((REQ, LANES), BF16),
        shape((GROUP, LANES), BF16),
        shape((GROUP, LANES), BF16),
        shape((4, PART, LANES), BF16),
    )
    return kernel_call(
        functools.partial(score_body, g),
        outs,
        (VMEM, VMEM, VMEM),
        scratch=[pltpu.VMEM((SPLIT, FOLD * LANES), BF16)],
        flops=1 << 29,
    )(arrived, slots, rel)


def split_body(kept_ref, other_ref, near_ref, far_ref):
    for half, ref in enumerate((near_ref, far_ref)):
        at = slice(2 * half, 2 * half + 2)
        ref[...] = (kept_ref[at].astype(F32) + other_ref[at].astype(F32)).astype(BF16)


def split_sum(kept, other):
    half = shape((2, PART, LANES), BF16)
    return kernel_call(split_body, (half, half), (VMEM, VMEM))(kept, other)


def add_body(a_ref, b_ref, c_ref, d_ref, near_ref, far_ref):
    near_ref[...] = (a_ref[...].astype(F32) + b_ref[...].astype(F32)).astype(BF16)
    far_ref[...] = (c_ref[...].astype(F32) + d_ref[...].astype(F32)).astype(BF16)


def added(*parts):
    half = shape((2, PART, LANES), BF16)
    return kernel_call(add_body, (half, half), (VMEM,) * 4)(*parts)


def coef_body(a_ref, b_ref, c_ref, d_ref, out_ref):
    for half, (left, right) in enumerate(((a_ref, b_ref), (c_ref, d_ref))):
        for q in range(2):
            total = left[q].astype(F32) + right[q].astype(F32)
            at = 2 * half + q
            out_ref[at, :256, :] = (jax.nn.sigmoid(total[:256, :]) / NEG).astype(BF16)
            out_ref[at, 256:, :] = (-jax.nn.sigmoid(-total[256:, :])).astype(BF16)


def coefficients(*parts):
    return kernel_call(coef_body, shape((4, PART, LANES), BF16), (VMEM,) * 4)(*parts)


def grad_body(mine_ref, other_ref, rows0, query0, probe0, rows1, query1, probe1, *refs):
    rel_ref, ids_ref, grads_ref, relrow_ref, tail_c, head_c = refs
    ids = ids_ref[...]
    coded = jnp.concatenate([ids >> 6, ids & 63, ids, ids], axis=0)
    relrow_ref[2 * GROUP :, :] = coded.astype(F32).astype(BF16)
    groups = ((mine_ref, rows0, query0, probe0), (other_ref, rows1, query1, probe1))
    for g, (coef_ref, rows_ref, query_ref, probe_ref) in enumerate(groups):
        for q in range(4):
            at = slice(q * 64, (q + 1) * 64)
            for c in range(2):
                lanes = slice(c * LANES, (c + 1) * LANES)
                tail_c[at, lanes] = coef_ref[q, c * 64 : (c + 1) * 64, :]
                head_c[at, lanes] = coef_ref[q, (2 + c) * 64 : (3 + c) * 64, :]
        pos = [column(coef_ref[q, 256:PART, :].astype(F32)[:1, :]) for q in (0, 2)]
        pos = jnp.concatenate(pos, axis=0)
        head = rows_ref[:GROUP, :].astype(F32)
        tail = rows_ref[GROUP : 2 * GROUP, :].astype(F32)
        noise = rows_ref[2 * GROUP :, :]
        rel = rel_ref[g].astype(BF16).astype(F32)
        tail_pull = pos * tail + dot(tail_c[...], noise)
        head_pull = dot(head_c[...], noise)
        head_side = pos * head + head_pull
        head_grad = product(tail_pull, rel, -1.0)
        tail_grad = product(head_side, rel)
        noise_grad = dot(tail_c[...], query_ref[...], ((0,), (0,))) + dot(
            head_c[...], probe_ref[...], ((0,), (0,))
        )
        relrow_ref[g * GROUP : (g + 1) * GROUP, :] = (
            product(tail_pull, head, -1.0) + product(tail, head_pull, -1.0)
        ).astype(BF16)
        grads_ref[g, :GROUP, :] = head_grad.astype(BF16)
        grads_ref[g, GROUP : 2 * GROUP, :] = tail_grad.astype(BF16)
        grads_ref[g, 2 * GROUP :, :] = noise_grad.astype(BF16)


def gradients(mine, other, kept, sent, rel, rel_ids):
    outs = (shape((2, REQ, LANES), BF16), shape((2 * GROUP + 16, LANES), BF16))
    return kernel_call(
        grad_body,
        outs,
        (VMEM,) * 10,
        scratch=[pltpu.VMEM((GROUP, NEG), BF16), pltpu.VMEM((GROUP, NEG), BF16)],
        flops=1 << 29,
    )(mine, other, *kept, *sent, rel, rel_ids)


def pack_body(grads_ref, slots_ref, out_hbm, out_ref, wide, hot, sems):
    copies = []
    for g in range(2):
        for b in range(REQ // LANES):
            row = slots_ref[g, b : b + 1, :]
            at = slice(b * LANES, (b + 1) * LANES)
            wide[at, :] = fold(grads_ref[g, at, :].astype(F32), column(row) >> 9)
            hot[:, at] = one_hot_columns(row & (SPLIT - 1), SPLIT)
        for k in range(SPLIT // LANES):
            packed = dot(hot[k * LANES : (k + 1) * LANES, :], wide[...])
            for j in range(FOLD):
                piece = packed[:, j * LANES : (j + 1) * LANES].astype(BF16)
                first = j * 8 + k * 2
                out_ref[g, first : first + 2] = piece.reshape(2, CAP, LANES)
        copies.append(started(out_ref.at[g], out_hbm.at[:, g * CAP : (g + 1) * CAP, :], sems.at[g]))
    for copy in copies:
        copy.wait()


def pack(grads, slots):
    return kernel_call(
        pack_body,
        shape((OWNERS, 2 * CAP, LANES), BF16),
        (VMEM, VMEM),
        scratch=[
            pltpu.VMEM((2, OWNERS, CAP, LANES), BF16),
            pltpu.VMEM((REQ, FOLD * LANES), BF16),
            pltpu.VMEM((SPLIT, REQ), BF16),
            pltpu.SemaphoreType.DMA((2,)),
        ],
        out_specs=HBM,
        flops=1 << 30,
    )(grads, slots)


def accumulate_body(
    ids_ref, back_hbm, reg_hbm, hot_hbm, total_hbm, square_ref,
    back_ref, reg_ref, hot, wide, total_ref, sems,
):
    pieces = 4
    step = OWNERS // pieces
    width = step * LANES
    backs, hots = [], []
    for k in range(pieces):
        at = slice(k * step, (k + 1) * step)
        backs.append(started(back_hbm.at[at], back_ref.at[at], sems.at[k]))
        at = slice(k * width, (k + 1) * width)
        hots.append(started(hot_hbm.at[:, at], hot.at[:, at], sems.at[pieces + k]))
    reg_copy = started(reg_hbm, reg_ref, sems.at[2 * pieces])
    for k in range(pieces):
        backs[k].wait()

        def spread_rows(i, _, k=k):
            at = k * step + i
            row = ids_ref[pl.ds(at, 1), :] - 1
            wide[pl.ds(pl.multiple_of(at * LANES, LANES), LANES), :] = fold(
                back_ref[at].astype(F32), column(row) >> 9
            )
            return 0

        lax.fori_loop(0, step, spread_rows, 0, unroll=4)
    for k in range(pieces):
        hots[k].wait()
    reg_copy.wait()

    def leave(m, j):
        at = pl.ds(pl.multiple_of(j * SPLIT + m * LANES, LANES), LANES)
        return pltpu.make_async_copy(total_ref.at[at], total_hbm.at[at], sems.at[9 + 4 * m + j])

    def sum_rows(m, _):
        at = pl.ds(pl.multiple_of(m * LANES, LANES), LANES)
        packed = dot(hot[at, :], wide[...])
        for j in range(FOLD):
            at = pl.ds(pl.multiple_of(j * SPLIT + m * LANES, LANES), LANES)
            total = packed[:, j * LANES : (j + 1) * LANES] + reg_ref[at, :]
            total_ref[at, :] = total
            square_ref[pl.ds(j * FOLD + m, 1), :] = jnp.sum(
                jnp.transpose(total * total), axis=0, keepdims=True
            )
            leave(m, j).start()
        return 0

    lax.fori_loop(0, SPLIT // LANES, sum_rows, 0, unroll=2)
    for m in range(SPLIT // LANES):
        for j in range(FOLD):
            leave(m, j).wait()


def accumulate(ids, back, reg, hot):
    rows = FOLD * SPLIT
    pairs = OWNERS * LANES
    return kernel_call(
        accumulate_body,
        (shape((rows, LANES), F32), shape((rows // LANES, LANES), F32)),
        (VMEM, HBM, HBM, HBM),
        scratch=[
            pltpu.VMEM((OWNERS, LANES, LANES), BF16),
            pltpu.VMEM((rows, LANES), F32),
            pltpu.VMEM((SPLIT, pairs), BF16),
            pltpu.VMEM((pairs, FOLD * LANES), BF16),
            pltpu.VMEM((rows, LANES), F32),
            pltpu.SemaphoreType.DMA((25,)),
        ],
        out_specs=(HBM, VMEM),
        flops=1 << 31,
        limit=24,
    )(ids, back, reg, hot)


def step_body(table_hbm, total_hbm, state_ref, square_ref, out_hbm, table_ref, total_ref, sems):
    pieces = 4
    rows = table_ref.shape[0] // pieces
    tables, totals, outs = [], [], []
    for k in range(pieces):
        at = slice(k * rows, (k + 1) * rows)
        tables.append(started(table_hbm.at[at], table_ref.at[at], sems.at[3 * k]))
        totals.append(started(total_hbm.at[at], total_ref.at[at], sems.at[3 * k + 1]))
    count = table_ref.shape[0] // LANES
    scale = LEARN_RATE / lax.sqrt(state_ref[...] + square_ref[:count, :] / (2 * RANK))
    for k in range(pieces):
        tables[k].wait()
        totals[k].wait()
        for b in range(k * rows // LANES, (k + 1) * rows // LANES):
            at = slice(b * LANES, (b + 1) * LANES)
            table_ref[at, :] = table_ref[at, :] - total_ref[at, :] * column(scale[b : b + 1, :])
        at = slice(k * rows, (k + 1) * rows)
        outs.append(started(table_ref.at[at], out_hbm.at[at], sems.at[3 * k + 2]))
    for copy in outs:
        copy.wait()


def entity_step(table, total, state, square):
    return kernel_call(
        step_body,
        shape(table.shape, F32),
        (HBM, HBM, VMEM, VMEM),
        scratch=[
            pltpu.VMEM(table.shape, F32),
            pltpu.VMEM(table.shape, F32),
            pltpu.SemaphoreType.DMA((12,)),
        ],
        out_specs=HBM,
    )(table, total, state, square)


def rel_sum_body(e_ref, *refs):
    rows, outs, wide, hot, total = refs[:4], refs[4:12], refs[12], refs[13], refs[14]
    y = e_ref[0] >> 3
    z = e_ref[0] & 7
    for s in range(4):
        coded = rows[s][2 * GROUP :, :].astype(F32)
        ids = (coded[:4] * 64.0 + coded[4:8]).astype(I32) - y * 1024
        for b in range(4):
            row = ids[b : b + 1, :]
            inside = (row >= 0) & (row < 1024)
            low = jnp.where(inside, row & 255, -1)
            at = slice(s * 512 + b * LANES, s * 512 + (b + 1) * LANES)
            wide[at, :] = fold(rows[s][b * LANES : (b + 1) * LANES, :].astype(F32), column(row) >> 8)
            hot[:, at] = one_hot_columns(low, 256)
    packed = dot(hot[...], wide[...]).astype(BF16)
    for k in range(8):
        total[k] = packed[
            (k % 2) * LANES : (k % 2 + 1) * LANES, (k // 2) * LANES : (k // 2 + 1) * LANES
        ]
    for s in range(8):
        outs[s][...] = total[(z + s) & 7]


def rel_sum(e, rows):
    return kernel_call(
        rel_sum_body,
        tuple(shape((LANES, LANES), BF16) for _ in range(8)),
        (SMEM,) + (VMEM,) * 4,
        scratch=[
            pltpu.VMEM((2048, FOLD * LANES), BF16),
            pltpu.VMEM((256, 2048), BF16),
            pltpu.VMEM((8, LANES, LANES), BF16),
        ],
        flops=1 << 29,
    )(e, *rows)


def rel_total_body(*refs):
    out_hbm, total_ref, sems = refs[8:]
    total = refs[0][...].astype(F32)
    for ref in refs[1:8]:
        total += ref[...].astype(F32)
    total_ref[...] = total.astype(BF16)
    for copy in [started(total_ref, out_hbm.at[k], sems.at[k]) for k in range(8)]:
        copy.wait()


def rel_total(parts):
    return kernel_call(
        rel_total_body,
        shape((8, LANES, LANES), BF16),
        (VMEM,) * 8,
        scratch=[pltpu.VMEM((LANES, LANES), BF16), pltpu.SemaphoreType.DMA((8,))],
        out_specs=HBM,
    )(*parts)


def squares_body(total_ref, out_ref):
    for k in range(8):
        total = total_ref[k].astype(F32)
        out_ref[k : k + 1, :] = jnp.sum(jnp.transpose(total * total), axis=0, keepdims=True)


def squares_of(total):
    return kernel_call(squares_body, shape((8, LANES), F32), (VMEM,))(total)


def rel_step_body(e_ref, table_ref, state_ref, *refs):
    square_refs, (out_hbm, out_ref, sems) = refs[4:8], refs[8:]
    y = e_ref[0] >> 3
    copies = []
    for s in range(4):
        quarter = (y + 4 - s) & 3
        state = state_ref[pl.ds(pl.multiple_of(quarter * 8, 8), 8), :]
        square = square_refs[s][...]
        scale = LEARN_RATE / lax.sqrt(state + square / (2 * RANK))
        for k in range(8):
            at = pl.ds(pl.multiple_of(quarter * 1024 + k * LANES, LANES), LANES)
            grad = refs[s][k].astype(F32)
            out_ref[at, :] = table_ref[at, :] - grad * column(scale[k : k + 1, :])
        at = pl.ds(pl.multiple_of(quarter * 1024, 1024), 1024)
        copies.append(started(out_ref.at[at], out_hbm.at[at], sems.at[s]))
    for copy in copies:
        copy.wait()


def rel_step(e, table, state, parts, squares):
    return kernel_call(
        rel_step_body,
        shape(table.shape, F32),
        (SMEM,) + (VMEM,) * 10,
        scratch=[pltpu.VMEM(table.shape, F32), pltpu.SemaphoreType.DMA((4,))],
        out_specs=HBM,
        flops=1 << 20,
    )(e, table, state, *parts, *squares)


Z_GROUPS = [[y * Z + z for z in range(Z)] for y in range(Y)]


def y_turn(s):
    return [(y * Z + z, (y + s) % Y * Z + z) for y in range(Y) for z in range(Z)]


def z_turn(s):
    return [(y * Z + z, y * Z + (z + s) % Z) for y in range(Y) for z in range(Z)]


X_MIRROR = [(x * 2 + c, (X - 1 - x) * 2 + c) for x in range(X) for c in range(2)]


def flip(bit):
    return [(i, i ^ bit) for i in range(X * CORES)]


def around(array, axis, turn, count):
    return [array] + [lax.ppermute(array, axis, turn(s)) for s in range(1, count)]


def scattered(parts, axis, turn):
    return [parts[0]] + [lax.ppermute(p, axis, turn(s)) for s, p in enumerate(parts) if s]


def summed_over_dim(values):
    for turn in (flip(1), flip(2), X_MIRROR):
        received = lax.ppermute(values, "dim", turn)
        values = values + received
    return values


def per_device(entities, ent_state, buckets, relations, rel_state, triples, negatives):
    rows_here = entities.shape[0]
    e = lax.axis_index("ent").reshape(1)
    core = (lax.axis_index("dim") & 1).reshape(1)
    slots, out_ids, rel_ids = place(core, triples, negatives)
    table = fold_table(entities)
    ids = lax.all_to_all(out_ids, "ent", 0, 0, tiled=True)
    arrived = lax.all_to_all(look_up(ids, table), "ent", 0, 0, tiled=True)
    rel = jnp.take(relations, rel_ids.reshape(-1), axis=0, mode="clip")
    rel = rel.reshape(2, GROUP, LANES)
    slots, rel = lax.optimization_barrier((slots, rel))

    *sent, partial = score(1, arrived, slots, rel)
    swapped = lax.ppermute(partial, "dim", flip(1))
    *kept, partial = score(0, arrived, slots, rel)
    near, far = split_sum(partial, swapped)
    near, far = added(
        near, lax.ppermute(near, "dim", flip(2)), far, lax.ppermute(far, "dim", X_MIRROR)
    )
    coef = coefficients(
        near, lax.ppermute(near, "dim", X_MIRROR), far, lax.ppermute(far, "dim", flip(2))
    )
    coef_other = lax.ppermute(coef, "dim", flip(1))
    grads, rel_rows = gradients(coef, coef_other, kept, sent, rel, rel_ids)
    packed, ids = lax.optimization_barrier((pack(grads, slots), ids))
    hot = spread(ids)
    flat = ids.reshape(-1) - 1
    counts = jnp.sum(
        (flat[:, None] == jnp.arange(rows_here, dtype=I32)[None, :]).astype(F32), axis=0
    )
    weight = REG_WEIGHT * (buckets.astype(F32) + 1.0) * counts
    reg = weight[:, None] * 3.0 * entities * jnp.abs(entities)
    near_rows = around(rel_rows, "ent", y_turn, Y)
    returned = lax.all_to_all(packed, "ent", 0, 0, tiled=True)
    parts = rel_sum(e, near_rows)
    parts = scattered(parts, "ent", z_turn)
    total, reg, hot = lax.optimization_barrier((rel_total(parts), reg, hot))
    joined = lax.all_to_all(total, "ent", 0, 0, tiled=True, axis_index_groups=Z_GROUPS)
    near_totals = around(joined, "ent", y_turn, Y)
    ent_total, ent_square = accumulate(ids, returned, reg, hot)
    squares = jnp.concatenate([ent_square, squares_of(joined)], axis=0)
    squares = summed_over_dim(squares)
    rel_squares = around(squares[rows_here // LANES :], "ent", y_turn, Y)
    new_relations = rel_step(
        e, relations, rel_state.reshape(OWNERS, LANES), near_totals, rel_squares
    )
    new_entities = entity_step(
        entities, ent_total, ent_state.reshape(rows_here // LANES, LANES), squares
    )
    return (new_entities, new_relations)


def solution(mesh):
    placed = (
        P("ent", "dim"),
        P("ent"),
        P("ent"),
        P(None, "dim"),
        P(),
        P(None, "ent"),
        P("ent", None),
    )
    return jax.shard_map(
        per_device,
        mesh=mesh,
        in_specs=placed,
        out_specs=(P("ent", "dim"), P(None, "dim")),
        check_vma=False,
    )
```
